512 devices in a mesh: wide: 128 (over z, y, core), narrow: 4 (over x).
Axes of the slice: x: 4, y: 4, z: 16, core: 2. Of those that a mesh axis runs over, the one named last changes fastest.
Arguments:
- trace_guess: float32 [128, 4, 16, 128, 128], P('wide', 'narrow'), may hold values from -6 to 6
- trace_rhs: float32 [128, 4, 16, 128, 128], P('wide', 'narrow'), may hold values from -6 to 6
- block_inverse: bfloat16 [128, 4, 16, 128, 128], P('wide', 'narrow')
- coupling: bfloat16 [128, 4, 16, 2, 128, 128], P('wide', 'narrow'), may hold values from -0.1875 to 0.1875
- block_neighbours: int32 [128, 4, 16, 2], P('wide', 'narrow'), may hold values from 0 to 23
- block_send: int32 [128, 4, 4, 2], P('wide', 'narrow'), may hold values from 0 to 15
- cell_faces: int32 [128, 4, 6, 2048], P('wide', 'narrow'), may hold values from 0 to 3071
- face_coeff: float32 [128, 4, 6, 2048], P('wide', 'narrow'), may hold values from 0.2 to 2
- cell_source: float32 [128, 4, 2048], P('wide', 'narrow'), may hold values from -6 to 6
- cell_neighbours: int32 [128, 4, 6, 2048], P('wide', 'narrow'), may hold values from 0 to 3071, as said below
- upwind_flags: int32 [128, 4, 6, 2048], P('wide', 'narrow'), may hold values 0 or 1
- cell_send: int32 [128, 4, 4, 256], P('wide', 'narrow'), may hold values from 0 to 2047
- saturation: float32 [128, 4, 4, 2048], P('wide', 'narrow'), may hold values from -3 to 3
- step_ratio: float32 [128, 4, 2048], P('wide', 'narrow'), may hold values from 0.05 to 0.2
Outputs:
- traces: float32 [128, 4, 16, 128, 128], P('wide', 'narrow')
- saturation_next: float32 [128, 4, 4, 2048], P('wide', 'narrow')
The draws below stay inside these ranges and needn't reach their ends.
Inputs may be any that keep to these rules, and one draw needn't show every extreme that they name: `cell_neighbours`: faces 0 to 3 (f) index either an own cell (below 2048) or a cell of their own side's range, 2048 + f * 256 to 2048 + (f + 1) * 256 - 1; faces 4 and 5 index own cells only.
All inputs are finite; a program needn't handle non-finite values. No bound on the sum of `upwind_flags` on one device may be relied on, other than what follows from the above.
Results may differ from the reference program's by a relative error of at most 0.003.
Values may be sent and summed in bfloat16 or wider, within the bound.
A program may use at most 64 MiB of HBM per device.

```python
import math
import jax
import jax.numpy as jnp
from jax import lax

F = 128
NB = 16
HB = 2
K = 2
R = 128
NC = 2048
HC = 256
N_WIDE = 128
N_NARROW = 4


def draw_block_inverse(key, part):
    first, second = jax.random.split(jax.random.fold_in(key, 11))
    shape = (N_WIDE, N_NARROW, NB, F, F)
    diagonal = jnp.exp(jax.random.uniform(first, shape[:-1], jnp.float32, math.log(0.15), math.log(0.6)))
    off_part = jax.random.normal(second, shape, jnp.float32) * (0.3 / math.sqrt(F))
    identity = (lax.broadcasted_iota(jnp.int32, (F, F), 0) == lax.broadcasted_iota(jnp.int32, (F, F), 1)).astype(jnp.float32)
    return (off_part + identity * diagonal[..., None]).astype(jnp.bfloat16)


def draw_cell_neighbours(key, part):
    first, second, third = jax.random.split(jax.random.fold_in(key, 23), 3)
    shape = (N_WIDE, N_NARROW, 6, NC)
    local = jax.random.randint(first, shape, 0, NC)
    offset = jax.random.randint(second, shape, 0, HC)
    face = lax.broadcasted_iota(jnp.int32, shape, 2)
    chosen = jax.random.randint(third, shape, 0, 2) * (face < 4).astype(jnp.int32)
    remote = NC + face * HC + offset
    return jnp.where(chosen == 1, remote, local).astype(jnp.int32)


def plant(result, own_key, least, high):
    longest = result.shape.index(max(result.shape))
    spots = []
    for shift in (0, 1):
        where = [jax.random.randint(jax.random.fold_in(own_key, axis), (), 0, length) for axis, length in enumerate(result.shape)]
        where[longest] = (where[longest] + shift) % result.shape[longest]
        spots.append(tuple(where))
    return result.at[spots[0]].set(least).at[spots[1]].set(high)


def steps_of(rng, shape, shards, least, largest):
    level, own = 1.0, jax.random.fold_in(rng, 6)
    for axis_at, parts in shards:
        steps = jnp.exp(jax.random.uniform(jax.random.fold_in(own, axis_at), (parts,), jnp.float32, least / len(shards), largest / len(shards)))
        level = level * jnp.repeat(steps, shape[axis_at] // parts).reshape([-1 if axis == axis_at else 1 for axis in range(len(shape))])
    return level


def gaussian(own_key, dims, spread, reach, shards=(), kind=jnp.bfloat16):
    values = spread * jax.random.normal(own_key, dims, jnp.float32)
    if shards:
        values = values * steps_of(own_key, dims, shards, -0.22, 0.18)
    return jnp.clip(values, -reach, reach).astype(kind)


def setup_inputs(seed: int = 0) -> dict:
    streams_of = jax.random.split(jax.random.key(seed), 15)
    trace_guess = gaussian(streams_of[0], (N_WIDE, N_NARROW, NB, R, F), 1.0, 6.0, ((0, 128), (1, 4)), jnp.float32)
    trace_rhs = gaussian(streams_of[1], (N_WIDE, N_NARROW, NB, R, F), 1.0, 6.0, ((0, 128), (1, 4)), jnp.float32)
    block_inverse = draw_block_inverse(jax.random.fold_in(streams_of[14], 71), 0)
    coupling = gaussian(streams_of[3], (N_WIDE, N_NARROW, NB, K, F, F), (8 * F) ** -0.5, 0.1875, ((0, 128), (1, 4)))
    block_neighbours = plant(jax.random.randint(streams_of[4], (N_WIDE, N_NARROW, NB, K), 0, NB + 4 * HB), jax.random.fold_in(streams_of[4], 1), 0, (NB + 4 * HB) - 1).astype(jnp.int32)
    block_send = plant(jax.random.randint(streams_of[5], (N_WIDE, N_NARROW, 4, HB), 0, NB), jax.random.fold_in(streams_of[5], 1), 0, NB - 1).astype(jnp.int32)
    cell_faces = plant(jax.random.randint(streams_of[6], (N_WIDE, N_NARROW, 6, NC), 0, (NB + 4 * HB) * F), jax.random.fold_in(streams_of[6], 1), 0, ((NB + 4 * HB) * F) - 1).astype(jnp.int32)
    face_coeff = jnp.clip(jnp.exp(math.log(2.0) - 2.3025851 * jax.random.uniform(streams_of[7], (N_WIDE, N_NARROW, 6, NC), jnp.float32) ** steps_of(streams_of[7], (N_WIDE, N_NARROW, 6, NC), ((0, 128), (1, 4)), -0.2, 0.2)), 0.2, 2.0)
    cell_source = gaussian(streams_of[8], (N_WIDE, N_NARROW, NC), 1.0, 6.0, ((0, 128), (1, 4)), jnp.float32)
    cell_neighbours = draw_cell_neighbours(jax.random.fold_in(streams_of[14], 71), 0)
    upwind_flags = plant((jax.random.randint(streams_of[10], (N_WIDE, N_NARROW, 6, NC), 0, 2) < 1).astype(jnp.int32), jax.random.fold_in(streams_of[10], 1), 0, 1)
    cell_send = plant(jax.random.randint(streams_of[11], (N_WIDE, N_NARROW, 4, HC), 0, NC), jax.random.fold_in(streams_of[11], 1), 0, NC - 1).astype(jnp.int32)
    saturation = gaussian(streams_of[12], (N_WIDE, N_NARROW, 4, NC), 0.5, 3.0, ((0, 128), (1, 4)), jnp.float32)
    step_ratio = jnp.clip(jnp.exp(math.log(0.2) - 1.3862944 * jax.random.uniform(streams_of[13], (N_WIDE, N_NARROW, NC), jnp.float32) ** steps_of(streams_of[13], (N_WIDE, N_NARROW, NC), ((0, 128), (1, 4)), -0.2, 0.2)), 0.05, 0.2)
    return dict(trace_guess=trace_guess, trace_rhs=trace_rhs, block_inverse=block_inverse, coupling=coupling, block_neighbours=block_neighbours, block_send=block_send, cell_faces=cell_faces, face_coeff=face_coeff, cell_source=cell_source, cell_neighbours=cell_neighbours, upwind_flags=upwind_flags, cell_send=cell_send, saturation=saturation, step_ratio=step_ratio)


def receive(send_data):
    zero_wide = jnp.zeros_like(send_data[:1, :, 0])
    west = jnp.concatenate([zero_wide, send_data[:-1, :, 1]], 0)
    east = jnp.concatenate([send_data[1:, :, 0], zero_wide], 0)
    zero_narrow = jnp.zeros_like(send_data[:, :1, 2])
    south = jnp.concatenate([zero_narrow, send_data[:, :-1, 3]], 1)
    north = jnp.concatenate([send_data[:, 1:, 2], zero_narrow], 1)
    return jnp.stack([west, east, south, north], 2)


def picked(values, index):
    return jax.vmap(jax.vmap(lambda x, i: x[i]))(values, index)


def smooth(extended, inverse, couple, links, rhs):
    near = extended[links]
    coupled = jnp.einsum("bkij,bkrj->bri", couple.astype(jnp.float32), near.astype(jnp.float32))
    resid = (rhs - coupled).astype(jnp.bfloat16)
    return jnp.einsum("bij,brj->bri", inverse.astype(jnp.float32), resid.astype(jnp.float32))


def smooth_slice(items):
    return jax.vmap(smooth)(*items)


def reference(trace_guess, trace_rhs, block_inverse, coupling, block_neighbours, block_send, cell_faces, face_coeff, cell_source, cell_neighbours, upwind_flags, cell_send, saturation, step_ratio):
    n_wide, n_narrow = trace_guess.shape[0], trace_guess.shape[1]
    sends = block_send.reshape(n_wide, n_narrow, 4 * HB)
    current = trace_guess.astype(jnp.bfloat16)
    fresh = trace_guess
    for sweep in range(2):
        outgoing = picked(current, sends).reshape(n_wide, n_narrow, 4, HB, R, F)
        arrived = receive(outgoing).reshape(n_wide, n_narrow, 4 * HB, R, F)
        extended = jnp.concatenate([current, arrived], 2)
        fresh = lax.map(smooth_slice, (extended, block_inverse, coupling, block_neighbours, trace_rhs))
        current = fresh.astype(jnp.bfloat16)
    first_column = current[:, :, :, 0, :]
    outgoing = picked(first_column, sends).reshape(n_wide, n_narrow, 4, HB * F)
    arrived = receive(outgoing).reshape(n_wide, n_narrow, 4 * HB * F)
    face_values = jnp.concatenate([first_column.reshape(n_wide, n_narrow, NB * F), arrived], 2).astype(jnp.float32)
    face_trace = picked(face_values, cell_faces)
    total = jnp.sum(face_coeff, 2)
    pressure = (cell_source + jnp.sum(face_coeff * face_trace, 2)) / total
    flux = face_coeff * (pressure[:, :, None, :] - face_trace)
    cell_out = jax.vmap(jax.vmap(lambda s, c: jnp.transpose(s[:, c], (1, 0, 2))))(saturation, cell_send)
    cell_in = receive(cell_out)
    cell_in = jnp.transpose(cell_in, (0, 1, 3, 2, 4)).reshape(n_wide, n_narrow, 4, 4 * HC)
    ext_sat = jnp.concatenate([saturation, cell_in], 3)
    across_modes = jax.vmap(jax.vmap(lambda e, idx: e[:, idx]))(ext_sat, cell_neighbours)
    flows = []
    for face in range(6):
        axis_mode = face // 2 + 1
        sign = -1.0 if face % 2 == 0 else 1.0
        own = saturation[:, :, 0] + sign * saturation[:, :, axis_mode]
        across = across_modes[:, :, 0, face] - sign * across_modes[:, :, axis_mode, face]
        upwind = jnp.where(upwind_flags[:, :, face] == 1, own, across)
        flows.append(flux[:, :, face] * upwind)
    flow = jnp.stack(flows, 2)
    modes = [saturation[:, :, 0] - step_ratio * jnp.sum(flow, 2)]
    for axis_mode in range(1, 4):
        low, high = 2 * axis_mode - 2, 2 * axis_mode - 1
        volume = 0.5 * (flux[:, :, high] - flux[:, :, low]) * saturation[:, :, 0]
        modes.append(saturation[:, :, axis_mode] + 3.0 * step_ratio * (volume - (flow[:, :, high] - flow[:, :, low])))
    return fresh, jnp.stack(modes, 2)
```

```python
import functools

import jax
import jax.numpy as jnp
from jax import lax
from jax.experimental import pallas as pl
from jax.experimental.pallas import tpu as pltpu
from jax.sharding import PartitionSpec as P

MESH = pl.DeviceIdType.MESH
LANES = 128
CHUNKS = ((0, 64), (64, 64))

OPPOSITE = (1, 0, 3, 2)


def nt_dot(a, b):
    return lax.dot_general(a, b, (((1,), (1,)), ((), ())), preferred_element_type=jnp.float32)


def pick_lanes(index, rows):
    low = index % LANES
    group = index // LANES
    result = jnp.zeros(index.shape, jnp.float32)
    for at, row in enumerate(rows):
        spread = jnp.broadcast_to(row, index.shape)
        taken = jnp.take_along_axis(spread, low, axis=1, mode="promise_in_bounds")
        result = jnp.where(group == at, taken, result)
    return result


def kernel(
    n_wide,
    n_narrow,
    links,
    sends,
    guess_hbm,
    rhs_hbm,
    inverse_hbm,
    couple_hbm,
    faces_hbm,
    coeff_hbm,
    source_hbm,
    near_hbm,
    flags_hbm,
    outbound_hbm,
    modes_hbm,
    ratio_hbm,
    traces_out,
    modes_out,
    guess,
    rhs,
    inverse,
    couple,
    faces,
    coeff,
    source,
    near,
    flags,
    outbound,
    modes,
    ratio,
    traces,
    modes_next,
    tables,
    cell_table,
    cell_out,
    cell_in,
    face_own,
    face_out,
    face_in,
    upwind,
    *rest,
):
    count = len(CHUNKS)
    first_ext, rest = rest[:count], rest[count:]
    second_ext, rest = rest[:count], rest[count:]
    second_own, rest = rest[:count], rest[count:]
    first_out, rest = rest[:count], rest[count:]
    second_out, rest = rest[:count], rest[count:]
    load_sem, store_sem, send_sem, recv_sem = rest
    blocks = guess.shape[0]
    halo = sends.shape[0]

    i = lax.axis_index("wide")
    j = lax.axis_index("narrow")
    there = (i > 0, i < n_wide - 1, j > 0, j < n_narrow - 1)
    device = ((i - 1, j), (i + 1, j), (i, j - 1), (i, j + 1))

    loads = []
    for at, (src, dst) in enumerate(
        (
            (guess_hbm, guess),
            (modes_hbm, modes),
            (outbound_hbm, outbound),
            (couple_hbm, couple),
            (rhs_hbm, rhs),
            (inverse_hbm, inverse),
            (near_hbm, near),
            (flags_hbm, flags),
            (faces_hbm, faces),
            (coeff_hbm, coeff),
            (source_hbm, source),
            (ratio_hbm, ratio),
        )
    ):
        copy = pltpu.make_async_copy(src, dst, load_sem.at[at])
        copy.start()
        loads.append(copy)

    barrier = pltpu.get_barrier_semaphore()
    for side in range(4):

        @pl.when(there[side])
        def _():
            pl.semaphore_signal(barrier, inc=1, device_id=device[side], device_id_type=MESH)

    def remote(src, dst, slot, side):
        return pltpu.make_async_remote_copy(
            src_ref=src,
            dst_ref=dst,
            send_sem=send_sem.at[slot, side],
            recv_sem=recv_sem.at[slot, side],
            device_id=device[side],
            device_id_type=MESH,
        )

    def start(slot, source_of, target_of):
        for side in range(4):

            @pl.when(there[side])
            def _():
                remote(source_of(side), target_of(OPPOSITE[side]), slot, side).start()

    def wait_sent(slot, source_of, target_of):
        for side in range(4):

            @pl.when(there[side])
            def _():
                remote(source_of(side), target_of(OPPOSITE[side]), slot, side).wait_send()

    def wait_arrived(slot, source_of, target_of):
        for side in range(4):

            @pl.when(there[side])
            def _():
                remote(source_of(side), target_of(side), slot, OPPOSITE[side]).wait_recv()

    def block_refs(outgoing, extended):
        return (
            lambda side: outgoing.at[pl.ds(side * halo, halo)],
            lambda side: extended.at[pl.ds(blocks + side * halo, halo)],
        )

    for part in range(count):
        for side in range(4):

            @pl.when(jnp.logical_not(there[side]))
            def _():
                at = pl.ds(blocks + side * halo, halo)
                empty = jnp.zeros((halo,) + first_ext[part].shape[1:], jnp.bfloat16)
                first_ext[part][at] = empty
                second_ext[part][at] = empty

    for side in range(4):

        @pl.when(jnp.logical_not(there[side]))
        def _():
            cell_in[side] = jnp.zeros(cell_in.shape[1:], jnp.float32)
            face_in[side] = jnp.zeros(face_in.shape[1:], jnp.float32)

    loads[0].wait()
    for part, (low, size) in enumerate(CHUNKS):
        for side in range(4):
            for h in range(halo):
                picked = guess[sends[h, side], low : low + size, :]
                first_out[part][side * halo + h] = picked.astype(jnp.bfloat16)
    neighbours = sum(x.astype(jnp.int32) for x in there)
    pl.semaphore_wait(barrier, neighbours)
    for part in range(count):
        start(part, *block_refs(first_out[part], first_ext[part]))

    cell_slot, face_slot = 2 * count, 2 * count + 1
    loads[1].wait()
    loads[2].wait()
    groups = modes.shape[0] // 4
    mode = [modes[pl.ds(m, groups, stride=4), :] for m in range(4)]
    for face in range(6):
        slope = mode[face // 2 + 1]
        table = mode[0] + slope if face % 2 == 0 else mode[0] - slope
        tables[face] = table
        if face < 4:
            cell_table[pl.ds(OPPOSITE[face], groups, stride=8), :] = table
            cell_table[pl.ds(OPPOSITE[face] + 4, groups, stride=8), :] = table
    index = outbound[...]
    low_part, high_part = index % LANES, index // LANES
    sent = jnp.zeros(index.shape, jnp.float32)
    for at in range(groups):
        taken = jnp.take_along_axis(
            cell_table[8 * at : 8 * at + 8, :], low_part, axis=1, mode="promise_in_bounds"
        )
        sent = jnp.where(high_part == at, taken, sent)
    for side in range(4):
        for h in range(2):
            cell_out[side, h : h + 1, :] = sent[4 * h + side : 4 * h + side + 1, :]
    cell_refs = (lambda side: cell_out.at[side], lambda side: cell_in.at[side])
    start(cell_slot, *cell_refs)

    for part, (low, size) in enumerate(CHUNKS):
        for b in range(blocks):
            first_ext[part][b] = guess[b, low : low + size, :].astype(jnp.bfloat16)

    loads[6].wait()
    loads[7].wait()
    wait_arrived(cell_slot, *cell_refs)
    for face in range(6):
        at = slice(face * groups, (face + 1) * groups)
        index = near[at, :]
        own = mode[0] - mode[face // 2 + 1] if face % 2 == 0 else mode[0] + mode[face // 2 + 1]
        rows = [tables[face, g : g + 1, :] for g in range(groups)]
        if face < 4:
            rows = rows + [cell_in[face, h : h + 1, :] for h in range(2)]
            index = jnp.where(index < groups * LANES, index, index - face * 2 * LANES)
        across = pick_lanes(index, rows)
        upwind[at, :] = jnp.where(flags[at, :] == 1, own, across)

    def smooth(extended, low, size, b):
        pair = jnp.concatenate([extended[links[0, b]], extended[links[1, b]]], axis=1)
        weight = jnp.concatenate([couple[b, 0], couple[b, 1]], axis=1)
        coupled = nt_dot(pair, weight)
        resid = (rhs[b, low : low + size, :] - coupled).astype(jnp.bfloat16)
        return nt_dot(resid, inverse[b])

    loads[3].wait()
    loads[4].wait()
    loads[5].wait()
    for part, (low, size) in enumerate(CHUNKS):
        wait_arrived(part, *block_refs(first_out[part], first_ext[part]))
        for b in range(blocks):
            new = smooth(first_ext[part], low, size, b).astype(jnp.bfloat16)
            second_own[part][b] = new
            second_ext[part][b] = new
        for side in range(4):
            for h in range(halo):
                second_out[part][side * halo + h] = second_own[part][sends[h, side]]
        start(count + part, *block_refs(second_out[part], second_ext[part]))

    face_refs = (lambda side: face_out.at[side], lambda side: face_in.at[side])
    stores = []
    for part, (low, size) in enumerate(CHUNKS):
        wait_arrived(count + part, *block_refs(second_out[part], second_ext[part]))
        for b in range(blocks):
            new = smooth(second_ext[part], low, size, b)
            traces[b, low : low + size, :] = new
            if part == 0:
                face_own[b] = new[0:1, :].astype(jnp.bfloat16).astype(jnp.float32)
        if part == 0:
            for side in range(4):
                for h in range(halo):
                    face_out[side, h : h + 1, :] = face_own[sends[h, side]]
            start(face_slot, *face_refs)
        copy = pltpu.make_async_copy(
            traces.at[:, pl.ds(low, size), :], traces_out.at[:, pl.ds(low, size), :], store_sem.at[part]
        )
        copy.start()
        stores.append(copy)

    for at in range(8, 12):
        loads[at].wait()
    wait_arrived(face_slot, *face_refs)
    rows = [face_own[b] for b in range(blocks)]
    rows = rows + [face_in[side, h : h + 1, :] for side in range(4) for h in range(halo)]
    face_trace = pick_lanes(faces[...], rows)
    weights = [coeff[f * groups : (f + 1) * groups, :] for f in range(6)]
    values = [face_trace[f * groups : (f + 1) * groups, :] for f in range(6)]
    total = sum(weights[1:], weights[0])
    weighted = [w * v for w, v in zip(weights, values)]
    pressure = (source[...] + sum(weighted[1:], weighted[0])) / total
    flux = [w * (pressure - v) for w, v in zip(weights, values)]
    flow = [flux[f] * upwind[f * groups : (f + 1) * groups, :] for f in range(6)]
    step = ratio[...]
    modes_next[pl.ds(0, groups, stride=4), :] = mode[0] - step * sum(flow[1:], flow[0])
    for m in range(1, 4):
        lo, hi = 2 * m - 2, 2 * m - 1
        volume = 0.5 * (flux[hi] - flux[lo]) * mode[0]
        modes_next[pl.ds(m, groups, stride=4), :] = mode[m] + 3.0 * step * (
            volume - (flow[hi] - flow[lo])
        )
    copy = pltpu.make_async_copy(modes_next, modes_out, store_sem.at[count])
    copy.start()
    stores.append(copy)

    for part in range(count):
        wait_sent(part, *block_refs(first_out[part], first_ext[part]))
        wait_sent(count + part, *block_refs(second_out[part], second_ext[part]))
    wait_sent(cell_slot, *cell_refs)
    wait_sent(face_slot, *face_refs)
    for copy in stores:
        copy.wait()


def per_device(
    n_wide,
    n_narrow,
    trace_guess,
    trace_rhs,
    block_inverse,
    coupling,
    block_neighbours,
    block_send,
    cell_faces,
    face_coeff,
    cell_source,
    cell_neighbours,
    upwind_flags,
    cell_send,
    saturation,
    step_ratio,
):
    blocks, rows, width = trace_guess.shape[2:]
    halo = block_send.shape[3]
    cells = saturation.shape[3]
    groups = cells // LANES
    side_groups = cell_send.shape[3] // LANES

    def by_tile(x):
        modes, length = x.shape[2:]
        return x.reshape(modes, length // LANES, LANES).transpose(1, 0, 2).reshape(-1, LANES)

    operands = (
        block_neighbours[0, 0].T,
        block_send[0, 0].T,
        trace_guess[0, 0],
        trace_rhs[0, 0],
        block_inverse[0, 0],
        coupling[0, 0],
        cell_faces.reshape(-1, LANES),
        face_coeff.reshape(-1, LANES),
        cell_source.reshape(-1, LANES),
        cell_neighbours.reshape(-1, LANES),
        upwind_flags.reshape(-1, LANES),
        by_tile(cell_send),
        by_tile(saturation),
        step_ratio.reshape(-1, LANES),
    )
    f32, bf16 = jnp.float32, jnp.bfloat16
    extended = blocks + 4 * halo
    slots = 2 * len(CHUNKS) + 2
    scratch = [pltpu.VMEM(x.shape, x.dtype) for x in operands[2:]]
    scratch += [
        pltpu.VMEM((blocks, rows, width), f32),
        pltpu.VMEM((4 * groups, LANES), f32),
        pltpu.VMEM((6, groups, LANES), f32),
        pltpu.VMEM((8 * groups, LANES), f32),
        pltpu.VMEM((4, side_groups, LANES), f32),
        pltpu.VMEM((4, side_groups, LANES), f32),
        pltpu.VMEM((blocks, 1, width), f32),
        pltpu.VMEM((4, halo, width), f32),
        pltpu.VMEM((4, halo, width), f32),
        pltpu.VMEM((6 * groups, LANES), f32),
    ]
    for leading in (extended, extended, blocks, 4 * halo, 4 * halo):
        scratch += [pltpu.VMEM((leading, size, width), bf16) for _, size in CHUNKS]
    scratch += [
        pltpu.SemaphoreType.DMA((12,)),
        pltpu.SemaphoreType.DMA((len(CHUNKS) + 1,)),
        pltpu.SemaphoreType.DMA((slots, 4)),
        pltpu.SemaphoreType.DMA((slots, 4)),
    ]
    traces, modes = pl.pallas_call(
        functools.partial(kernel, n_wide, n_narrow),
        out_shape=(
            jax.ShapeDtypeStruct((blocks, rows, width), f32),
            jax.ShapeDtypeStruct((4 * groups, LANES), f32),
        ),
        in_specs=[pl.BlockSpec(memory_space=pltpu.SMEM)] * 2
        + [pl.BlockSpec(memory_space=pltpu.HBM)] * 12,
        out_specs=(pl.BlockSpec(memory_space=pl.ANY),) * 2,
        scratch_shapes=scratch,
        compiler_params=pltpu.CompilerParams(
            collective_id=0, has_side_effects=True, vmem_limit_bytes=32 * 1024 * 1024
        ),
        name="smooth_and_section",
    )(*operands)
    modes = modes.reshape(groups, 4, LANES).transpose(1, 0, 2).reshape(1, 1, 4, cells)
    return traces[None, None], modes


def solution(mesh):
    def placed(rank):
        return P("wide", "narrow", *([None] * (rank - 2)))

    ranks = (5, 5, 5, 6, 4, 4, 4, 4, 3, 4, 4, 4, 4, 3)
    return jax.shard_map(
        functools.partial(per_device, mesh.shape["wide"], mesh.shape["narrow"]),
        mesh=mesh,
        in_specs=tuple(placed(rank) for rank in ranks),
        out_specs=(placed(5), placed(4)),
        check_vma=False,
    )
```

```python
import functools

import jax
import jax.numpy as jnp
from jax import lax
from jax.experimental import pallas as pl
from jax.experimental.pallas import tpu as pltpu
from jax.sharding import PartitionSpec as P

MESH = pl.DeviceIdType.MESH
LANES = 128
VMEM_LIMIT = 48 * 1024 * 1024
CHUNKS = ((0, 16), (16, 112))

OPPOSITE = (1, 0, 3, 2)


def nt_dot(a, b):
    return lax.dot_general(a, b, (((1,), (1,)), ((), ())), preferred_element_type=jnp.float32)


def pick_lanes(index, rows):
    low = index % LANES
    group = index // LANES
    result = jnp.zeros(index.shape, jnp.float32)
    for at, row in enumerate(rows):
        spread = jnp.broadcast_to(row, index.shape)
        taken = jnp.take_along_axis(spread, low, axis=1, mode="promise_in_bounds")
        result = jnp.where(group == at, taken, result)
    return result


def kernel(
    n_wide,
    n_narrow,
    links_hbm,
    sends_hbm,
    guess_hbm,
    rhs_hbm,
    inverse_hbm,
    couple_hbm,
    faces_hbm,
    coeff_hbm,
    source_hbm,
    near_hbm,
    flags_hbm,
    outbound_hbm,
    modes_hbm,
    ratio_hbm,
    traces,
    modes_next,
    links,
    sends,
    rhs,
    inverse,
    couple,
    faces,
    coeff,
    source,
    near,
    flags,
    outbound,
    modes,
    ratio,
    tables,
    cell_table,
    cell_out,
    cell_in,
    face_own,
    face_out,
    face_in,
    upwind,
    *rest,
):
    count = len(CHUNKS)
    guess, rest = rest[:count], rest[count:]
    first_ext, rest = rest[:count], rest[count:]
    second_ext, rest = rest[:count], rest[count:]
    second_own, rest = rest[:count], rest[count:]
    first_out, rest = rest[:count], rest[count:]
    second_out, rest = rest[:count], rest[count:]
    load_sem, send_sem, recv_sem = rest
    blocks = rhs.shape[0]
    halo = sends.shape[0]

    i = lax.axis_index("wide")
    j = lax.axis_index("narrow")
    there = (i > 0, i < n_wide - 1, j > 0, j < n_narrow - 1)
    device = ((i - 1, j), (i + 1, j), (i, j - 1), (i, j + 1))

    barrier = pltpu.get_barrier_semaphore()
    for side in range(4):

        @pl.when(there[side])
        def _():
            pl.semaphore_signal(barrier, inc=1, device_id=device[side], device_id_type=MESH)

    def load(at, src, dst):
        copy = pltpu.make_async_copy(src, dst, load_sem.at[at])
        copy.start()
        return copy

    load_sends = load(0, sends_hbm, sends)
    load_guess = []
    for part, (low, size) in enumerate(CHUNKS):
        load_guess.append(load(1 + part, guess_hbm.at[:, pl.ds(low, size)], guess[part]))
    load_links = load(1 + count, links_hbm, links)
    loads = [
        load(2 + count + at, src, dst)
        for at, (src, dst) in enumerate(
            (
                (modes_hbm, modes),
                (outbound_hbm, outbound),
                (couple_hbm, couple),
                (rhs_hbm, rhs),
                (inverse_hbm, inverse),
                (near_hbm, near),
                (flags_hbm, flags),
                (faces_hbm, faces),
                (coeff_hbm, coeff),
                (source_hbm, source),
                (ratio_hbm, ratio),
            )
        )
    ]
    load_modes, load_outbound, load_couple, load_rhs, load_inverse, load_near, load_flags = loads[:7]
    load_cells = loads[7:]

    def remote(src, dst, slot, side):
        return pltpu.make_async_remote_copy(
            src_ref=src,
            dst_ref=dst,
            send_sem=send_sem.at[slot, side],
            recv_sem=recv_sem.at[slot, side],
            device_id=device[side],
            device_id_type=MESH,
        )

    def start(slot, source_of, target_of):
        for side in range(4):

            @pl.when(there[side])
            def _():
                remote(source_of(side), target_of(OPPOSITE[side]), slot, side).start()

    def wait_sent(slot, source_of, target_of):
        for side in range(4):

            @pl.when(there[side])
            def _():
                remote(source_of(side), target_of(OPPOSITE[side]), slot, side).wait_send()

    def wait_arrived(slot, source_of, target_of):
        for side in range(4):

            @pl.when(there[side])
            def _():
                remote(source_of(side), target_of(side), slot, OPPOSITE[side]).wait_recv()

    def block_refs(outgoing, extended):
        return (
            lambda side: outgoing.at[pl.ds(side * halo, halo)],
            lambda side: extended.at[pl.ds(blocks + side * halo, halo)],
        )

    for part in range(count):
        for side in range(4):

            @pl.when(jnp.logical_not(there[side]))
            def _():
                at = pl.ds(blocks + side * halo, halo)
                empty = jnp.zeros((halo,) + first_ext[part].shape[1:], jnp.bfloat16)
                first_ext[part][at] = empty
                second_ext[part][at] = empty

    for side in range(4):

        @pl.when(jnp.logical_not(there[side]))
        def _():
            cell_in[side] = jnp.zeros(cell_in.shape[1:], jnp.float32)
            face_in[side] = jnp.zeros(face_in.shape[1:], jnp.float32)

    load_sends.wait()
    for part, (low, size) in enumerate(CHUNKS):
        load_guess[part].wait()
        for side in range(4):
            for h in range(halo):
                picked = guess[part][sends[h, side]]
                first_out[part][side * halo + h] = picked.astype(jnp.bfloat16)
        if part == 0:
            pl.semaphore_wait(barrier, sum(x.astype(jnp.int32) for x in there))
        start(part, *block_refs(first_out[part], first_ext[part]))

    cell_slot, face_slot = 2 * count, 2 * count + 1
    load_modes.wait()
    load_outbound.wait()
    groups = modes.shape[0] // 4
    mode = [modes[pl.ds(m, groups, stride=4), :] for m in range(4)]
    for face in range(6):
        slope = mode[face // 2 + 1]
        table = mode[0] + slope if face % 2 == 0 else mode[0] - slope
        tables[face] = table
        if face < 4:
            cell_table[pl.ds(OPPOSITE[face], groups, stride=8), :] = table
            cell_table[pl.ds(OPPOSITE[face] + 4, groups, stride=8), :] = table
    index = outbound[...]
    low_part, high_part = index % LANES, index // LANES
    sent = jnp.zeros(index.shape, jnp.float32)
    for at in range(groups):
        taken = jnp.take_along_axis(
            cell_table[8 * at : 8 * at + 8, :], low_part, axis=1, mode="promise_in_bounds"
        )
        sent = jnp.where(high_part == at, taken, sent)
    for side in range(4):
        for h in range(2):
            cell_out[side, h : h + 1, :] = sent[4 * h + side : 4 * h + side + 1, :]
    cell_refs = (lambda side: cell_out.at[side], lambda side: cell_in.at[side])
    start(cell_slot, *cell_refs)

    for part, (low, size) in enumerate(CHUNKS):
        for b in range(blocks):
            first_ext[part][b] = guess[part][b].astype(jnp.bfloat16)

    load_near.wait()
    load_flags.wait()
    wait_arrived(cell_slot, *cell_refs)
    for face in range(6):
        at = slice(face * groups, (face + 1) * groups)
        index = near[at, :]
        own = mode[0] - mode[face // 2 + 1] if face % 2 == 0 else mode[0] + mode[face // 2 + 1]
        rows = [tables[face, g : g + 1, :] for g in range(groups)]
        if face < 4:
            rows = rows + [cell_in[face, h : h + 1, :] for h in range(2)]
            index = jnp.where(index < groups * LANES, index, index - face * 2 * LANES)
        across = pick_lanes(index, rows)
        upwind[at, :] = jnp.where(flags[at, :] == 1, own, across)

    def smooth(extended, low, size, b):
        pair = jnp.concatenate([extended[links[0, b]], extended[links[1, b]]], axis=1)
        weight = jnp.concatenate([couple[b, 0], couple[b, 1]], axis=1)
        coupled = nt_dot(pair, weight)
        resid = (rhs[b, low : low + size, :] - coupled).astype(jnp.bfloat16)
        return nt_dot(resid, inverse[b])

    load_links.wait()
    load_couple.wait()
    load_rhs.wait()
    load_inverse.wait()
    for part, (low, size) in enumerate(CHUNKS):
        wait_arrived(part, *block_refs(first_out[part], first_ext[part]))
        for b in range(blocks):
            new = smooth(first_ext[part], low, size, b).astype(jnp.bfloat16)
            second_own[part][b] = new
            second_ext[part][b] = new
        for side in range(4):
            for h in range(halo):
                second_out[part][side * halo + h] = second_own[part][sends[h, side]]
        start(count + part, *block_refs(second_out[part], second_ext[part]))

    face_refs = (lambda side: face_out.at[side], lambda side: face_in.at[side])
    for part, (low, size) in enumerate(CHUNKS):
        wait_arrived(count + part, *block_refs(second_out[part], second_ext[part]))
        for b in range(blocks):
            new = smooth(second_ext[part], low, size, b)
            traces[b, low : low + size, :] = new
            if part == 0:
                face_own[b] = new[0:1, :].astype(jnp.bfloat16).astype(jnp.float32)
        if part == 0:
            for side in range(4):
                for h in range(halo):
                    face_out[side, h : h + 1, :] = face_own[sends[h, side]]
            start(face_slot, *face_refs)

    for copy in load_cells:
        copy.wait()
    wait_arrived(face_slot, *face_refs)
    rows = [face_own[b] for b in range(blocks)]
    rows = rows + [face_in[side, h : h + 1, :] for side in range(4) for h in range(halo)]
    face_trace = pick_lanes(faces[...], rows)
    weights = [coeff[f * groups : (f + 1) * groups, :] for f in range(6)]
    values = [face_trace[f * groups : (f + 1) * groups, :] for f in range(6)]
    total = sum(weights[1:], weights[0])
    weighted = [w * v for w, v in zip(weights, values)]
    pressure = (source[...] + sum(weighted[1:], weighted[0])) / total
    flux = [w * (pressure - v) for w, v in zip(weights, values)]
    flow = [flux[f] * upwind[f * groups : (f + 1) * groups, :] for f in range(6)]
    step = ratio[...]
    modes_next[pl.ds(0, groups, stride=4), :] = mode[0] - step * sum(flow[1:], flow[0])
    for m in range(1, 4):
        lo, hi = 2 * m - 2, 2 * m - 1
        volume = 0.5 * (flux[hi] - flux[lo]) * mode[0]
        modes_next[pl.ds(m, groups, stride=4), :] = mode[m] + 3.0 * step * (
            volume - (flow[hi] - flow[lo])
        )
    for part in range(count):
        wait_sent(part, *block_refs(first_out[part], first_ext[part]))
        wait_sent(count + part, *block_refs(second_out[part], second_ext[part]))
    wait_sent(cell_slot, *cell_refs)
    wait_sent(face_slot, *face_refs)


def write_back(traces, modes, traces_out, modes_out, sem):
    copies = [
        pltpu.make_async_copy(traces, traces_out, sem.at[0]),
        pltpu.make_async_copy(modes, modes_out, sem.at[1]),
    ]
    for copy in copies:
        copy.start()
    for copy in copies:
        copy.wait()


def per_device(
    n_wide,
    n_narrow,
    trace_guess,
    trace_rhs,
    block_inverse,
    coupling,
    block_neighbours,
    block_send,
    cell_faces,
    face_coeff,
    cell_source,
    cell_neighbours,
    upwind_flags,
    cell_send,
    saturation,
    step_ratio,
):
    blocks, rows, width = trace_guess.shape[2:]
    halo = block_send.shape[3]
    cells = saturation.shape[3]
    groups = cells // LANES
    side_groups = cell_send.shape[3] // LANES

    def by_tile(x):
        modes, length = x.shape[2:]
        return x.reshape(modes, length // LANES, LANES).transpose(1, 0, 2).reshape(-1, LANES)

    operands = (
        block_neighbours[0, 0].T,
        block_send[0, 0].T,
        trace_guess[0, 0],
        trace_rhs[0, 0],
        block_inverse[0, 0],
        coupling[0, 0],
        cell_faces.reshape(-1, LANES),
        face_coeff.reshape(-1, LANES),
        cell_source.reshape(-1, LANES),
        cell_neighbours.reshape(-1, LANES),
        upwind_flags.reshape(-1, LANES),
        by_tile(cell_send),
        by_tile(saturation),
        step_ratio.reshape(-1, LANES),
    )
    f32, bf16 = jnp.float32, jnp.bfloat16
    extended = blocks + 4 * halo
    slots = 2 * len(CHUNKS) + 2
    scratch = [pltpu.SMEM(x.shape, x.dtype) for x in operands[:2]]
    scratch += [pltpu.VMEM(x.shape, x.dtype) for x in operands[3:]]
    scratch += [
        pltpu.VMEM((6, groups, LANES), f32),
        pltpu.VMEM((8 * groups, LANES), f32),
        pltpu.VMEM((4, side_groups, LANES), f32),
        pltpu.VMEM((4, side_groups, LANES), f32),
        pltpu.VMEM((blocks, 1, width), f32),
        pltpu.VMEM((4, halo, width), f32),
        pltpu.VMEM((4, halo, width), f32),
        pltpu.VMEM((6 * groups, LANES), f32),
    ]
    scratch += [pltpu.VMEM((blocks, size, width), f32) for _, size in CHUNKS]
    for leading in (extended, extended, blocks, 4 * halo, 4 * halo):
        scratch += [pltpu.VMEM((leading, size, width), bf16) for _, size in CHUNKS]
    scratch += [
        pltpu.SemaphoreType.DMA((13 + len(CHUNKS),)),
        pltpu.SemaphoreType.DMA((slots, 4)),
        pltpu.SemaphoreType.DMA((slots, 4)),
    ]
    shapes = ((blocks, rows, width), (4 * groups, LANES))
    results = pl.pallas_call(
        functools.partial(kernel, n_wide, n_narrow),
        out_shape=tuple(pltpu.VMEM(shape, f32) for shape in shapes),
        in_specs=[pl.BlockSpec(memory_space=pltpu.HBM)] * len(operands),
        out_specs=(pl.BlockSpec(memory_space=pltpu.VMEM),) * 2,
        scratch_shapes=scratch,
        compiler_params=pltpu.CompilerParams(
            collective_id=0, has_side_effects=True, vmem_limit_bytes=VMEM_LIMIT
        ),
        name="smooth_and_section",
    )(*(pltpu.with_memory_space_constraint(x, pltpu.HBM) for x in operands))
    traces, modes = pl.pallas_call(
        write_back,
        out_shape=tuple(jax.ShapeDtypeStruct(shape, f32) for shape in shapes),
        in_specs=[pl.BlockSpec(memory_space=pl.ANY)] * 2,
        out_specs=(pl.BlockSpec(memory_space=pl.ANY),) * 2,
        scratch_shapes=[pltpu.SemaphoreType.DMA((2,))],
        name="write_back",
    )(*(pltpu.with_memory_space_constraint(x, pltpu.VMEM) for x in results))
    modes = modes.reshape(groups, 4, LANES).transpose(1, 0, 2).reshape(1, 1, 4, cells)
    return traces[None, None], modes


def solution(mesh):
    def placed(rank):
        return P("wide", "narrow", *([None] * (rank - 2)))

    ranks = (5, 5, 5, 6, 4, 4, 4, 4, 3, 4, 4, 4, 4, 3)
    return jax.shard_map(
        functools.partial(per_device, mesh.shape["wide"], mesh.shape["narrow"]),
        mesh=mesh,
        in_specs=tuple(placed(rank) for rank in ranks),
        out_specs=(placed(5), placed(4)),
        check_vma=False,
    )
```

```python
import functools

import jax
import jax.numpy as jnp
from jax import lax
from jax.experimental import pallas as pl
from jax.experimental.pallas import tpu as pltpu
from jax.sharding import PartitionSpec as P

MESH = pl.DeviceIdType.MESH
LANES = 128
VMEM_LIMIT = 48 * 1024 * 1024
CHUNKS = ((0, 16), (16, 112))

OPPOSITE = (1, 0, 3, 2)


def nt_dot(a, b):
    return lax.dot_general(a, b, (((1,), (1,)), ((), ())), preferred_element_type=jnp.float32)


def pick_lanes(index, rows, first=0, result=None):
    low = index % LANES
    group = index // LANES
    if result is None:
        result = jnp.zeros(index.shape, jnp.float32)
    for at, row in enumerate(rows, first):
        spread = jnp.broadcast_to(row, index.shape)
        taken = jnp.take_along_axis(spread, low, axis=1, mode="promise_in_bounds")
        result = jnp.where(group == at, taken, result)
    return result


def kernel(
    n_wide,
    n_narrow,
    links_hbm,
    sends_hbm,
    guess_hbm,
    rhs_hbm,
    inverse_hbm,
    couple_hbm,
    faces_hbm,
    coeff_hbm,
    source_hbm,
    near_hbm,
    flags_hbm,
    outbound_hbm,
    modes_hbm,
    ratio_hbm,
    traces,
    modes_next,
    links,
    sends,
    rhs,
    inverse,
    couple,
    faces,
    coeff,
    source,
    near,
    flags,
    outbound,
    modes,
    ratio,
    tables,
    cell_table,
    cell_out,
    cell_in,
    face_own,
    face_out,
    face_in,
    upwind,
    *rest,
):
    count = len(CHUNKS)
    guess, rest = rest[:count], rest[count:]
    first_ext, rest = rest[:count], rest[count:]
    second_ext, rest = rest[:count], rest[count:]
    first_out, rest = rest[:count], rest[count:]
    second_out, rest = rest[:count], rest[count:]
    load_sem, send_sem, recv_sem = rest
    blocks = rhs.shape[0]
    halo = sends.shape[0]

    i = lax.axis_index("wide")
    j = lax.axis_index("narrow")
    there = (i > 0, i < n_wide - 1, j > 0, j < n_narrow - 1)
    device = ((i - 1, j), (i + 1, j), (i, j - 1), (i, j + 1))

    def load(at, src, dst):
        copy = pltpu.make_async_copy(src, dst, load_sem.at[at])
        copy.start()
        return copy

    load_sends = load(0, sends_hbm, sends)
    load_guess = []
    for part, (low, size) in enumerate(CHUNKS):
        load_guess.append(load(1 + part, guess_hbm.at[:, pl.ds(low, size)], guess[part]))

    barrier = pltpu.get_barrier_semaphore()
    for side in range(4):

        @pl.when(there[side])
        def _():
            pl.semaphore_signal(barrier, inc=1, device_id=device[side], device_id_type=MESH)

    def remote(src, dst, slot, side):
        return pltpu.make_async_remote_copy(
            src_ref=src,
            dst_ref=dst,
            send_sem=send_sem.at[slot, side],
            recv_sem=recv_sem.at[slot, side],
            device_id=device[side],
            device_id_type=MESH,
        )

    def start(slot, source_of, target_of):
        for side in range(4):

            @pl.when(there[side])
            def _():
                remote(source_of(side), target_of(OPPOSITE[side]), slot, side).start()

    def wait_sent(slot, source_of, target_of):
        for side in range(4):

            @pl.when(there[side])
            def _():
                remote(source_of(side), target_of(OPPOSITE[side]), slot, side).wait_send()

    def wait_arrived(slot, source_of, target_of):
        for side in range(4):

            @pl.when(there[side])
            def _():
                remote(source_of(side), target_of(side), slot, OPPOSITE[side]).wait_recv()

    def block_refs(outgoing, extended):
        return (
            lambda side: outgoing.at[pl.ds(side * halo, halo)],
            lambda side: extended.at[pl.ds(blocks + side * halo, halo)],
        )

    for part in range(count):
        for side in range(4):

            @pl.when(jnp.logical_not(there[side]))
            def _():
                at = pl.ds(blocks + side * halo, halo)
                empty = jnp.zeros((halo,) + first_ext[part].shape[1:], jnp.bfloat16)
                first_ext[part][at] = empty
                second_ext[part][at] = empty

    for side in range(4):

        @pl.when(jnp.logical_not(there[side]))
        def _():
            cell_in[side] = jnp.zeros(cell_in.shape[1:], jnp.float32)
            face_in[side] = jnp.zeros(face_in.shape[1:], jnp.float32)

    load_sends.wait()
    for part, (low, size) in enumerate(CHUNKS):
        load_guess[part].wait()
        for side in range(4):
            for h in range(halo):
                picked = guess[part][sends[h, side]]
                first_out[part][side * halo + h] = picked.astype(jnp.bfloat16)
        if part == 0:
            pl.semaphore_wait(barrier, sum(x.astype(jnp.int32) for x in there))
        start(part, *block_refs(first_out[part], first_ext[part]))
        if part == 0:
            load_links = load(1 + count, links_hbm, links)
            loads = [
                load(2 + count + at, src, dst)
                for at, (src, dst) in enumerate(
                    (
                        (couple_hbm, couple),
                        (inverse_hbm, inverse),
                        (rhs_hbm, rhs),
                        (modes_hbm, modes),
                        (outbound_hbm, outbound),
                        (near_hbm, near),
                        (flags_hbm, flags),
                        (faces_hbm, faces),
                        (coeff_hbm, coeff),
                        (source_hbm, source),
                        (ratio_hbm, ratio),
                    )
                )
            ]
    load_couple, load_inverse, load_rhs, load_modes, load_outbound, load_near, load_flags = loads[:7]
    load_cells = loads[7:]

    cell_slot, face_slot = 2 * count, 2 * count + 1
    load_modes.wait()
    load_outbound.wait()
    groups = modes.shape[0] // 4
    mode = [modes[pl.ds(m, groups, stride=4), :] for m in range(4)]
    for face in range(6):
        slope = mode[face // 2 + 1]
        table = mode[0] + slope if face % 2 == 0 else mode[0] - slope
        tables[face] = table
        if face < 4:
            cell_table[pl.ds(OPPOSITE[face], groups, stride=8), :] = table
            cell_table[pl.ds(OPPOSITE[face] + 4, groups, stride=8), :] = table
    index = outbound[...]
    low_part, high_part = index % LANES, index // LANES
    sent = jnp.zeros(index.shape, jnp.float32)
    for at in range(groups):
        taken = jnp.take_along_axis(
            cell_table[8 * at : 8 * at + 8, :], low_part, axis=1, mode="promise_in_bounds"
        )
        sent = jnp.where(high_part == at, taken, sent)
    for side in range(4):
        for h in range(2):
            cell_out[side, h : h + 1, :] = sent[4 * h + side : 4 * h + side + 1, :]
    cell_refs = (lambda side: cell_out.at[side], lambda side: cell_in.at[side])
    start(cell_slot, *cell_refs)

    for part, (low, size) in enumerate(CHUNKS):
        for b in range(blocks):
            first_ext[part][b] = guess[part][b].astype(jnp.bfloat16)

    def smooth(extended, low, size, b):
        pair = jnp.concatenate([extended[links[0, b]], extended[links[1, b]]], axis=1)
        weight = jnp.concatenate([couple[b, 0], couple[b, 1]], axis=1)
        coupled = nt_dot(pair, weight)
        resid = (rhs[b, low : low + size, :] - coupled).astype(jnp.bfloat16)
        return nt_dot(resid, inverse[b])

    load_links.wait()
    load_couple.wait()
    load_rhs.wait()
    load_inverse.wait()

    def listed(extended, low, size, out):
        for side in range(4):
            for h in range(halo):
                out(side, h, smooth(extended, low, size, sends[h, side]))

    for part, (low, size) in enumerate(CHUNKS):

        def keep(side, h, new):
            second_out[part][side * halo + h] = new.astype(jnp.bfloat16)

        wait_arrived(part, *block_refs(first_out[part], first_ext[part]))
        listed(first_ext[part], low, size, keep)
        start(count + part, *block_refs(second_out[part], second_ext[part]))
    for part, (low, size) in enumerate(CHUNKS):
        for b in range(blocks):
            second_ext[part][b] = smooth(first_ext[part], low, size, b).astype(jnp.bfloat16)

    load_near.wait()
    load_flags.wait()
    wait_arrived(cell_slot, *cell_refs)
    for face in range(6):
        at = slice(face * groups, (face + 1) * groups)
        index = near[at, :]
        own = mode[0] - mode[face // 2 + 1] if face % 2 == 0 else mode[0] + mode[face // 2 + 1]
        rows = [tables[face, g : g + 1, :] for g in range(groups)]
        if face < 4:
            rows = rows + [cell_in[face, h : h + 1, :] for h in range(2)]
            index = jnp.where(index < groups * LANES, index, index - face * 2 * LANES)
        across = pick_lanes(index, rows)
        upwind[at, :] = jnp.where(flags[at, :] == 1, own, across)

    def keep_row(side, h, new):
        face_out[side, h : h + 1, :] = new[0:1, :].astype(jnp.bfloat16).astype(jnp.float32)

    face_refs = (lambda side: face_out.at[side], lambda side: face_in.at[side])
    for part, (low, size) in enumerate(CHUNKS):
        wait_arrived(count + part, *block_refs(second_out[part], second_ext[part]))
        if part == 0:
            listed(second_ext[part], low, size, keep_row)
            start(face_slot, *face_refs)
        for b in range(blocks):
            new = smooth(second_ext[part], low, size, b)
            traces[b, low : low + size, :] = new
            if part == 0:
                face_own[b] = new[0:1, :].astype(jnp.bfloat16).astype(jnp.float32)

    for copy in load_cells:
        copy.wait()
    face_index = faces[...]
    face_trace = pick_lanes(face_index, [face_own[b] for b in range(blocks)])
    wait_arrived(face_slot, *face_refs)
    rows = [face_in[side, h : h + 1, :] for side in range(4) for h in range(halo)]
    face_trace = pick_lanes(face_index, rows, blocks, face_trace)
    weights = [coeff[f * groups : (f + 1) * groups, :] for f in range(6)]
    values = [face_trace[f * groups : (f + 1) * groups, :] for f in range(6)]
    total = sum(weights[1:], weights[0])
    weighted = [w * v for w, v in zip(weights, values)]
    pressure = (source[...] + sum(weighted[1:], weighted[0])) / total
    flux = [w * (pressure - v) for w, v in zip(weights, values)]
    flow = [flux[f] * upwind[f * groups : (f + 1) * groups, :] for f in range(6)]
    step = ratio[...]
    modes_next[pl.ds(0, groups, stride=4), :] = mode[0] - step * sum(flow[1:], flow[0])
    for m in range(1, 4):
        lo, hi = 2 * m - 2, 2 * m - 1
        volume = 0.5 * (flux[hi] - flux[lo]) * mode[0]
        modes_next[pl.ds(m, groups, stride=4), :] = mode[m] + 3.0 * step * (
            volume - (flow[hi] - flow[lo])
        )
    for part in range(count):
        wait_sent(part, *block_refs(first_out[part], first_ext[part]))
        wait_sent(count + part, *block_refs(second_out[part], second_ext[part]))
    wait_sent(cell_slot, *cell_refs)
    wait_sent(face_slot, *face_refs)


def write_back(traces, modes, traces_out, modes_out, sem):
    copies = [
        pltpu.make_async_copy(traces, traces_out, sem.at[0]),
        pltpu.make_async_copy(modes, modes_out, sem.at[1]),
    ]
    for copy in copies:
        copy.start()
    for copy in copies:
        copy.wait()


def per_device(
    n_wide,
    n_narrow,
    trace_guess,
    trace_rhs,
    block_inverse,
    coupling,
    block_neighbours,
    block_send,
    cell_faces,
    face_coeff,
    cell_source,
    cell_neighbours,
    upwind_flags,
    cell_send,
    saturation,
    step_ratio,
):
    blocks, rows, width = trace_guess.shape[2:]
    halo = block_send.shape[3]
    cells = saturation.shape[3]
    groups = cells // LANES
    side_groups = cell_send.shape[3] // LANES

    def by_tile(x):
        modes, length = x.shape[2:]
        return x.reshape(modes, length // LANES, LANES).transpose(1, 0, 2).reshape(-1, LANES)

    operands = (
        block_neighbours[0, 0].T,
        block_send[0, 0].T,
        trace_guess[0, 0],
        trace_rhs[0, 0],
        block_inverse[0, 0],
        coupling[0, 0],
        cell_faces.reshape(-1, LANES),
        face_coeff.reshape(-1, LANES),
        cell_source.reshape(-1, LANES),
        cell_neighbours.reshape(-1, LANES),
        upwind_flags.reshape(-1, LANES),
        by_tile(cell_send),
        by_tile(saturation),
        step_ratio.reshape(-1, LANES),
    )
    f32, bf16 = jnp.float32, jnp.bfloat16
    extended = blocks + 4 * halo
    slots = 2 * len(CHUNKS) + 2
    scratch = [pltpu.SMEM(x.shape, x.dtype) for x in operands[:2]]
    scratch += [pltpu.VMEM(x.shape, x.dtype) for x in operands[3:]]
    scratch += [
        pltpu.VMEM((6, groups, LANES), f32),
        pltpu.VMEM((8 * groups, LANES), f32),
        pltpu.VMEM((4, side_groups, LANES), f32),
        pltpu.VMEM((4, side_groups, LANES), f32),
        pltpu.VMEM((blocks, 1, width), f32),
        pltpu.VMEM((4, halo, width), f32),
        pltpu.VMEM((4, halo, width), f32),
        pltpu.VMEM((6 * groups, LANES), f32),
    ]
    scratch += [pltpu.VMEM((blocks, size, width), f32) for _, size in CHUNKS]
    for leading in (extended, extended, 4 * halo, 4 * halo):
        scratch += [pltpu.VMEM((leading, size, width), bf16) for _, size in CHUNKS]
    scratch += [
        pltpu.SemaphoreType.DMA((13 + len(CHUNKS),)),
        pltpu.SemaphoreType.DMA((slots, 4)),
        pltpu.SemaphoreType.DMA((slots, 4)),
    ]
    shapes = ((blocks, rows, width), (4 * groups, LANES))
    results = pl.pallas_call(
        functools.partial(kernel, n_wide, n_narrow),
        out_shape=tuple(pltpu.VMEM(shape, f32) for shape in shapes),
        in_specs=[pl.BlockSpec(memory_space=pltpu.HBM)] * len(operands),
        out_specs=(pl.BlockSpec(memory_space=pltpu.VMEM),) * 2,
        scratch_shapes=scratch,
        compiler_params=pltpu.CompilerParams(
            collective_id=0, has_side_effects=True, vmem_limit_bytes=VMEM_LIMIT
        ),
        name="smooth_and_section",
    )(*(pltpu.with_memory_space_constraint(x, pltpu.HBM) for x in operands))
    traces, modes = pl.pallas_call(
        write_back,
        out_shape=tuple(jax.ShapeDtypeStruct(shape, f32) for shape in shapes),
        in_specs=[pl.BlockSpec(memory_space=pl.ANY)] * 2,
        out_specs=(pl.BlockSpec(memory_space=pl.ANY),) * 2,
        scratch_shapes=[pltpu.SemaphoreType.DMA((2,))],
        name="write_back",
    )(*(pltpu.with_memory_space_constraint(x, pltpu.VMEM) for x in results))
    modes = modes.reshape(groups, 4, LANES).transpose(1, 0, 2).reshape(1, 1, 4, cells)
    return traces[None, None], modes


def solution(mesh):
    def placed(rank):
        return P("wide", "narrow", *([None] * (rank - 2)))

    ranks = (5, 5, 5, 6, 4, 4, 4, 4, 3, 4, 4, 4, 4, 3)
    return jax.shard_map(
        functools.partial(per_device, mesh.shape["wide"], mesh.shape["narrow"]),
        mesh=mesh,
        in_specs=tuple(placed(rank) for rank in ranks),
        out_specs=(placed(5), placed(4)),
        check_vma=False,
    )
```

```python
import functools

import jax
import jax.numpy as jnp
from jax import lax
from jax.experimental import pallas as pl
from jax.experimental.pallas import tpu as pltpu
from jax.sharding import PartitionSpec as P

MESH = pl.DeviceIdType.MESH
LANES = 128
VMEM_LIMIT = 48 * 1024 * 1024
CHUNKS = ((0, 16), (16, 112))

OPPOSITE = (1, 0, 3, 2)


def nt_dot(a, b):
    return lax.dot_general(a, b, (((1,), (1,)), ((), ())), preferred_element_type=jnp.float32)


def pick_lanes(index, rows, first=0, result=None):
    low = index % LANES
    group = index // LANES
    if result is None:
        result = jnp.zeros(index.shape, jnp.float32)
    for at, row in enumerate(rows, first):
        spread = jnp.broadcast_to(row, index.shape)
        taken = jnp.take_along_axis(spread, low, axis=1, mode="promise_in_bounds")
        result = jnp.where(group == at, taken, result)
    return result


def smooth_kernel(
    n_wide,
    n_narrow,
    links_hbm,
    sends_hbm,
    guess_hbm,
    rhs_hbm,
    inverse_hbm,
    couple_hbm,
    faces_hbm,
    coeff_hbm,
    source_hbm,
    near_hbm,
    flags_hbm,
    outbound_hbm,
    modes_hbm,
    ratio_hbm,
    traces,
    partial,
    face_rows,
    upwind,
    faces,
    coeff,
    source,
    modes,
    ratio,
    links,
    sends,
    rhs,
    inverse,
    couple,
    near,
    flags,
    outbound,
    tables,
    cell_table,
    cell_out,
    cell_in,
    face_own,
    face_out,
    face_in,
    *rest,
):
    count = len(CHUNKS)
    guess, rest = rest[:count], rest[count:]
    first_ext, rest = rest[:count], rest[count:]
    second_ext, rest = rest[:count], rest[count:]
    first_out, rest = rest[:count], rest[count:]
    second_out, rest = rest[:count], rest[count:]
    load_sem, send_sem, recv_sem = rest
    blocks = rhs.shape[0]
    halo = sends.shape[0]

    i = lax.axis_index("wide")
    j = lax.axis_index("narrow")
    there = (i > 0, i < n_wide - 1, j > 0, j < n_narrow - 1)
    device = ((i - 1, j), (i + 1, j), (i, j - 1), (i, j + 1))

    def load(at, src, dst):
        copy = pltpu.make_async_copy(src, dst, load_sem.at[at])
        copy.start()
        return copy

    load_sends = load(0, sends_hbm, sends)
    load_guess = []
    for part, (low, size) in enumerate(CHUNKS):
        load_guess.append(load(1 + part, guess_hbm.at[:, pl.ds(low, size)], guess[part]))

    barrier = pltpu.get_barrier_semaphore()
    for side in range(4):

        @pl.when(there[side])
        def _():
            pl.semaphore_signal(barrier, inc=1, device_id=device[side], device_id_type=MESH)

    def remote(src, dst, slot, side):
        return pltpu.make_async_remote_copy(
            src_ref=src,
            dst_ref=dst,
            send_sem=send_sem.at[slot, side],
            recv_sem=recv_sem.at[slot, side],
            device_id=device[side],
            device_id_type=MESH,
        )

    def start(slot, source_of, target_of):
        for side in range(4):

            @pl.when(there[side])
            def _():
                remote(source_of(side), target_of(OPPOSITE[side]), slot, side).start()

    def wait_sent(slot, source_of, target_of):
        for side in range(4):

            @pl.when(there[side])
            def _():
                remote(source_of(side), target_of(OPPOSITE[side]), slot, side).wait_send()

    def wait_arrived(slot, source_of, target_of):
        for side in range(4):

            @pl.when(there[side])
            def _():
                remote(source_of(side), target_of(side), slot, OPPOSITE[side]).wait_recv()

    def block_refs(outgoing, extended):
        return (
            lambda side: outgoing.at[pl.ds(side * halo, halo)],
            lambda side: extended.at[pl.ds(blocks + side * halo, halo)],
        )

    for part in range(count):
        for side in range(4):

            @pl.when(jnp.logical_not(there[side]))
            def _():
                at = pl.ds(blocks + side * halo, halo)
                empty = jnp.zeros((halo,) + first_ext[part].shape[1:], jnp.bfloat16)
                first_ext[part][at] = empty
                second_ext[part][at] = empty

    for side in range(4):

        @pl.when(jnp.logical_not(there[side]))
        def _():
            cell_in[side] = jnp.zeros(cell_in.shape[1:], jnp.float32)
            face_in[side] = jnp.zeros(face_in.shape[1:], jnp.float32)

    load_sends.wait()
    for part, (low, size) in enumerate(CHUNKS):
        load_guess[part].wait()
        for side in range(4):
            for h in range(halo):
                picked = guess[part][sends[h, side]]
                first_out[part][side * halo + h] = picked.astype(jnp.bfloat16)
        if part == 0:
            pl.semaphore_wait(barrier, sum(x.astype(jnp.int32) for x in there))
        start(part, *block_refs(first_out[part], first_ext[part]))
        if part == 0:
            load_links = load(1 + count, links_hbm, links)
            loads = [
                load(2 + count + at, src, dst)
                for at, (src, dst) in enumerate(
                    (
                        (couple_hbm, couple),
                        (inverse_hbm, inverse),
                        (rhs_hbm, rhs),
                        (modes_hbm, modes),
                        (outbound_hbm, outbound),
                        (near_hbm, near),
                        (flags_hbm, flags),
                        (faces_hbm, faces),
                        (coeff_hbm, coeff),
                        (source_hbm, source),
                        (ratio_hbm, ratio),
                    )
                )
            ]
    load_couple, load_inverse, load_rhs, load_modes, load_outbound, load_near, load_flags = loads[:7]
    load_cells = loads[7:]

    cell_slot, face_slot = 2 * count, 2 * count + 1
    load_modes.wait()
    load_outbound.wait()
    groups = modes.shape[0] // 4
    mode = [modes[pl.ds(m, groups, stride=4), :] for m in range(4)]
    for face in range(6):
        slope = mode[face // 2 + 1]
        table = mode[0] + slope if face % 2 == 0 else mode[0] - slope
        tables[face] = table
        if face < 4:
            cell_table[pl.ds(OPPOSITE[face], groups, stride=8), :] = table
            cell_table[pl.ds(OPPOSITE[face] + 4, groups, stride=8), :] = table
    index = outbound[...]
    low_part, high_part = index % LANES, index // LANES
    sent = jnp.zeros(index.shape, jnp.float32)
    for at in range(groups):
        taken = jnp.take_along_axis(
            cell_table[8 * at : 8 * at + 8, :], low_part, axis=1, mode="promise_in_bounds"
        )
        sent = jnp.where(high_part == at, taken, sent)
    for side in range(4):
        for h in range(2):
            cell_out[side, h : h + 1, :] = sent[4 * h + side : 4 * h + side + 1, :]
    cell_refs = (lambda side: cell_out.at[side], lambda side: cell_in.at[side])
    start(cell_slot, *cell_refs)

    for part, (low, size) in enumerate(CHUNKS):
        for b in range(blocks):
            first_ext[part][b] = guess[part][b].astype(jnp.bfloat16)

    def smooth(extended, low, size, b):
        pair = jnp.concatenate([extended[links[0, b]], extended[links[1, b]]], axis=1)
        weight = jnp.concatenate([couple[b, 0], couple[b, 1]], axis=1)
        coupled = nt_dot(pair, weight)
        resid = (rhs[b, low : low + size, :] - coupled).astype(jnp.bfloat16)
        return nt_dot(resid, inverse[b])

    load_links.wait()
    load_couple.wait()
    load_rhs.wait()
    load_inverse.wait()

    def listed(extended, low, size, out):
        for side in range(4):
            for h in range(halo):
                out(side, h, smooth(extended, low, size, sends[h, side]))

    for part, (low, size) in enumerate(CHUNKS):

        def keep(side, h, new):
            second_out[part][side * halo + h] = new.astype(jnp.bfloat16)

        wait_arrived(part, *block_refs(first_out[part], first_ext[part]))
        listed(first_ext[part], low, size, keep)
        start(count + part, *block_refs(second_out[part], second_ext[part]))
    for part, (low, size) in enumerate(CHUNKS):
        for b in range(blocks):
            second_ext[part][b] = smooth(first_ext[part], low, size, b).astype(jnp.bfloat16)

    load_near.wait()
    load_flags.wait()
    wait_arrived(cell_slot, *cell_refs)
    for face in range(6):
        at = slice(face * groups, (face + 1) * groups)
        index = near[at, :]
        own = mode[0] - mode[face // 2 + 1] if face % 2 == 0 else mode[0] + mode[face // 2 + 1]
        rows = [tables[face, g : g + 1, :] for g in range(groups)]
        if face < 4:
            rows = rows + [cell_in[face, h : h + 1, :] for h in range(2)]
            index = jnp.where(index < groups * LANES, index, index - face * 2 * LANES)
        across = pick_lanes(index, rows)
        upwind[at, :] = jnp.where(flags[at, :] == 1, own, across)

    def keep_row(side, h, new):
        face_out[side, h : h + 1, :] = new[0:1, :].astype(jnp.bfloat16).astype(jnp.float32)

    face_refs = (lambda side: face_out.at[side], lambda side: face_in.at[side])
    for part, (low, size) in enumerate(CHUNKS):
        wait_arrived(count + part, *block_refs(second_out[part], second_ext[part]))
        if part == 0:
            listed(second_ext[part], low, size, keep_row)
            start(face_slot, *face_refs)
        for b in range(blocks):
            new = smooth(second_ext[part], low, size, b)
            traces[b, low : low + size, :] = new
            if part == 0:
                face_own[b] = new[0:1, :].astype(jnp.bfloat16).astype(jnp.float32)

    for copy in load_cells:
        copy.wait()
    partial[...] = pick_lanes(faces[...], [face_own[b] for b in range(blocks)])
    wait_arrived(face_slot, *face_refs)
    for side in range(4):
        for h in range(halo):
            face_rows[side * halo + h : side * halo + h + 1, :] = face_in[side, h : h + 1, :]

    for part in range(count):
        wait_sent(part, *block_refs(first_out[part], first_ext[part]))
        wait_sent(count + part, *block_refs(second_out[part], second_ext[part]))
    wait_sent(cell_slot, *cell_refs)
    wait_sent(face_slot, *face_refs)


def section(
    blocks,
    traces,
    partial,
    face_rows,
    upwind,
    faces,
    coeff,
    source,
    modes,
    ratio,
    traces_out,
    modes_out,
    modes_next,
    sem,
):
    write_traces = pltpu.make_async_copy(traces, traces_out, sem.at[0])
    write_traces.start()
    rows = [face_rows[h : h + 1, :] for h in range(face_rows.shape[0])]
    face_trace = pick_lanes(faces[...], rows, blocks, partial[...])
    groups = source.shape[0]
    mode = [modes[pl.ds(m, groups, stride=4), :] for m in range(4)]
    weights = [coeff[f * groups : (f + 1) * groups, :] for f in range(6)]
    values = [face_trace[f * groups : (f + 1) * groups, :] for f in range(6)]
    total = sum(weights[1:], weights[0])
    weighted = [w * v for w, v in zip(weights, values)]
    pressure = (source[...] + sum(weighted[1:], weighted[0])) / total
    flux = [w * (pressure - v) for w, v in zip(weights, values)]
    flow = [flux[f] * upwind[f * groups : (f + 1) * groups, :] for f in range(6)]
    step = ratio[...]
    modes_next[pl.ds(0, groups, stride=4), :] = mode[0] - step * sum(flow[1:], flow[0])
    for m in range(1, 4):
        lo, hi = 2 * m - 2, 2 * m - 1
        volume = 0.5 * (flux[hi] - flux[lo]) * mode[0]
        modes_next[pl.ds(m, groups, stride=4), :] = mode[m] + 3.0 * step * (
            volume - (flow[hi] - flow[lo])
        )
    write_modes = pltpu.make_async_copy(modes_next, modes_out, sem.at[1])
    write_modes.start()
    write_traces.wait()
    write_modes.wait()


def per_device(
    n_wide,
    n_narrow,
    trace_guess,
    trace_rhs,
    block_inverse,
    coupling,
    block_neighbours,
    block_send,
    cell_faces,
    face_coeff,
    cell_source,
    cell_neighbours,
    upwind_flags,
    cell_send,
    saturation,
    step_ratio,
):
    blocks, rows, width = trace_guess.shape[2:]
    halo = block_send.shape[3]
    cells = saturation.shape[3]
    groups = cells // LANES
    side_groups = cell_send.shape[3] // LANES

    def by_tile(x):
        modes, length = x.shape[2:]
        return x.reshape(modes, length // LANES, LANES).transpose(1, 0, 2).reshape(-1, LANES)

    operands = (
        block_neighbours[0, 0].T,
        block_send[0, 0].T,
        trace_guess[0, 0],
        trace_rhs[0, 0],
        block_inverse[0, 0],
        coupling[0, 0],
        cell_faces.reshape(-1, LANES),
        face_coeff.reshape(-1, LANES),
        cell_source.reshape(-1, LANES),
        cell_neighbours.reshape(-1, LANES),
        upwind_flags.reshape(-1, LANES),
        by_tile(cell_send),
        by_tile(saturation),
        step_ratio.reshape(-1, LANES),
    )
    f32, bf16 = jnp.float32, jnp.bfloat16
    extended = blocks + 4 * halo
    slots = 2 * len(CHUNKS) + 2
    scratch = [pltpu.SMEM(x.shape, x.dtype) for x in operands[:2]]
    scratch += [pltpu.VMEM(operands[at].shape, operands[at].dtype) for at in (3, 4, 5, 9, 10, 11)]
    scratch += [
        pltpu.VMEM((6, groups, LANES), f32),
        pltpu.VMEM((8 * groups, LANES), f32),
        pltpu.VMEM((4, side_groups, LANES), f32),
        pltpu.VMEM((4, side_groups, LANES), f32),
        pltpu.VMEM((blocks, 1, width), f32),
        pltpu.VMEM((4, halo, width), f32),
        pltpu.VMEM((4, halo, width), f32),
    ]
    scratch += [pltpu.VMEM((blocks, size, width), f32) for _, size in CHUNKS]
    for leading in (extended, extended, 4 * halo, 4 * halo):
        scratch += [pltpu.VMEM((leading, size, width), bf16) for _, size in CHUNKS]
    scratch += [
        pltpu.SemaphoreType.DMA((13 + len(CHUNKS),)),
        pltpu.SemaphoreType.DMA((slots, 4)),
        pltpu.SemaphoreType.DMA((slots, 4)),
    ]
    cells_shape = (6 * groups, LANES)
    shapes = [(blocks, rows, width), cells_shape, (4 * halo, width), cells_shape]
    kept = [(shape, f32) for shape in shapes]
    kept += [(operands[at].shape, operands[at].dtype) for at in (6, 7, 8, 12, 13)]
    results = pl.pallas_call(
        functools.partial(smooth_kernel, n_wide, n_narrow),
        out_shape=tuple(pltpu.VMEM(*x) for x in kept),
        in_specs=[pl.BlockSpec(memory_space=pltpu.HBM)] * len(operands),
        out_specs=(pl.BlockSpec(memory_space=pltpu.VMEM),) * len(kept),
        scratch_shapes=scratch,
        compiler_params=pltpu.CompilerParams(
            collective_id=0, has_side_effects=True, vmem_limit_bytes=VMEM_LIMIT
        ),
        name="smooth",
    )(*(pltpu.with_memory_space_constraint(x, pltpu.HBM) for x in operands))
    traces, modes = pl.pallas_call(
        functools.partial(section, blocks),
        out_shape=(
            jax.ShapeDtypeStruct(shapes[0], f32),
            jax.ShapeDtypeStruct((4 * groups, LANES), f32),
        ),
        in_specs=[pl.BlockSpec(memory_space=pltpu.VMEM)] * len(kept),
        out_specs=(pl.BlockSpec(memory_space=pl.ANY),) * 2,
        scratch_shapes=[pltpu.VMEM((4 * groups, LANES), f32), pltpu.SemaphoreType.DMA((2,))],
        name="section",
    )(*(pltpu.with_memory_space_constraint(x, pltpu.VMEM) for x in results))
    modes = modes.reshape(groups, 4, LANES).transpose(1, 0, 2).reshape(1, 1, 4, cells)
    return traces[None, None], modes


def solution(mesh):
    def placed(rank):
        return P("wide", "narrow", *([None] * (rank - 2)))

    ranks = (5, 5, 5, 6, 4, 4, 4, 4, 3, 4, 4, 4, 4, 3)
    return jax.shard_map(
        functools.partial(per_device, mesh.shape["wide"], mesh.shape["narrow"]),
        mesh=mesh,
        in_specs=tuple(placed(rank) for rank in ranks),
        out_specs=(placed(5), placed(4)),
        check_vma=False,
    )
```

```python
import functools

import jax
import jax.numpy as jnp
from jax import lax
from jax.experimental import pallas as pl
from jax.experimental.pallas import tpu as pltpu
from jax.sharding import PartitionSpec as P

MESH = pl.DeviceIdType.MESH
LANES = 128
VMEM_LIMIT = 48 * 1024 * 1024
CHUNKS = ((0, 16), (16, 112))

OPPOSITE = (1, 0, 3, 2)


def nt_dot(a, b):
    return lax.dot_general(a, b, (((1,), (1,)), ((), ())), preferred_element_type=jnp.float32)


def pick_lanes(index, rows, first=0, result=None):
    low = index % LANES
    group = index // LANES
    if result is None:
        result = jnp.zeros(index.shape, jnp.float32)
    for at, row in enumerate(rows, first):
        spread = jnp.broadcast_to(row, index.shape)
        taken = jnp.take_along_axis(spread, low, axis=1, mode="promise_in_bounds")
        result = jnp.where(group == at, taken, result)
    return result


def smooth_kernel(
    n_wide,
    n_narrow,
    links_hbm,
    sends_hbm,
    guess_hbm,
    rhs_hbm,
    inverse_hbm,
    couple_hbm,
    faces_hbm,
    coeff_hbm,
    source_hbm,
    near_hbm,
    flags_hbm,
    outbound_hbm,
    modes_hbm,
    ratio_hbm,
    traces,
    partial,
    face_rows,
    upwind,
    faces,
    coeff,
    source,
    modes,
    ratio,
    links,
    sends,
    rhs,
    inverse,
    couple,
    near,
    flags,
    outbound,
    tables,
    cell_table,
    cell_out,
    cell_in,
    face_own,
    face_out,
    face_in,
    *rest,
):
    count = len(CHUNKS)
    guess, rest = rest[:count], rest[count:]
    first_ext, rest = rest[:count], rest[count:]
    second_ext, rest = rest[:count], rest[count:]
    first_out, rest = rest[:count], rest[count:]
    second_out, rest = rest[:count], rest[count:]
    load_sem, send_sem, recv_sem = rest
    blocks = rhs.shape[0]
    halo = sends.shape[0]

    i = lax.axis_index("wide")
    j = lax.axis_index("narrow")
    there = (i > 0, i < n_wide - 1, j > 0, j < n_narrow - 1)
    device = ((i - 1, j), (i + 1, j), (i, j - 1), (i, j + 1))

    def load(at, src, dst):
        copy = pltpu.make_async_copy(src, dst, load_sem.at[at])
        copy.start()
        return copy

    load_sends = load(0, sends_hbm, sends)
    load_guess = []
    for part, (low, size) in enumerate(CHUNKS):
        load_guess.append(load(1 + part, guess_hbm.at[:, pl.ds(low, size)], guess[part]))

    barrier = pltpu.get_barrier_semaphore()
    for side in range(4):

        @pl.when(there[side])
        def _():
            pl.semaphore_signal(barrier, inc=1, device_id=device[side], device_id_type=MESH)

    def remote(src, dst, slot, side):
        return pltpu.make_async_remote_copy(
            src_ref=src,
            dst_ref=dst,
            send_sem=send_sem.at[slot, side],
            recv_sem=recv_sem.at[slot, side],
            device_id=device[side],
            device_id_type=MESH,
        )

    def start(slot, source_of, target_of):
        for side in range(4):

            @pl.when(there[side])
            def _():
                remote(source_of(side), target_of(OPPOSITE[side]), slot, side).start()

    def wait_sent(slot, source_of, target_of):
        for side in range(4):

            @pl.when(there[side])
            def _():
                remote(source_of(side), target_of(OPPOSITE[side]), slot, side).wait_send()

    def wait_arrived(slot, source_of, target_of):
        for side in range(4):

            @pl.when(there[side])
            def _():
                remote(source_of(side), target_of(side), slot, OPPOSITE[side]).wait_recv()

    def block_refs(outgoing, extended):
        return (
            lambda side: outgoing.at[pl.ds(side * halo, halo)],
            lambda side: extended.at[pl.ds(blocks + side * halo, halo)],
        )

    for part in range(count):
        for side in range(4):

            @pl.when(jnp.logical_not(there[side]))
            def _():
                at = pl.ds(blocks + side * halo, halo)
                empty = jnp.zeros((halo,) + first_ext[part].shape[1:], jnp.bfloat16)
                first_ext[part][at] = empty
                second_ext[part][at] = empty

    for side in range(4):

        @pl.when(jnp.logical_not(there[side]))
        def _():
            cell_in[side] = jnp.zeros(cell_in.shape[1:], jnp.float32)
            face_in[side] = jnp.zeros(face_in.shape[1:], jnp.float32)

    load_sends.wait()
    for part, (low, size) in enumerate(CHUNKS):
        load_guess[part].wait()
        for side in range(4):
            for h in range(halo):
                picked = guess[part][sends[h, side]]
                first_out[part][side * halo + h] = picked.astype(jnp.bfloat16)
        if part == 0:
            pl.semaphore_wait(barrier, sum(x.astype(jnp.int32) for x in there))
        start(part, *block_refs(first_out[part], first_ext[part]))
        if part == 0:
            load_links = load(1 + count, links_hbm, links)
            loads = [
                load(2 + count + at, src, dst)
                for at, (src, dst) in enumerate(
                    (
                        (couple_hbm, couple),
                        (inverse_hbm, inverse),
                        (rhs_hbm, rhs),
                        (modes_hbm, modes),
                        (outbound_hbm, outbound),
                        (near_hbm, near),
                        (flags_hbm, flags),
                        (faces_hbm, faces),
                        (coeff_hbm, coeff),
                        (source_hbm, source),
                        (ratio_hbm, ratio),
                    )
                )
            ]
    load_couple, load_inverse, load_rhs, load_modes, load_outbound, load_near, load_flags = loads[:7]
    load_cells = loads[7:]

    cell_slot, face_slot = 2 * count, 2 * count + 1
    load_modes.wait()
    load_outbound.wait()
    groups = modes.shape[0] // 4
    mode = [modes[pl.ds(m, groups, stride=4), :] for m in range(4)]
    for face in range(6):
        slope = mode[face // 2 + 1]
        table = mode[0] + slope if face % 2 == 0 else mode[0] - slope
        tables[face] = table
        if face < 4:
            cell_table[pl.ds(OPPOSITE[face], groups, stride=8), :] = table
            cell_table[pl.ds(OPPOSITE[face] + 4, groups, stride=8), :] = table
    index = outbound[...]
    low_part, high_part = index % LANES, index // LANES
    sent = jnp.zeros(index.shape, jnp.float32)
    for at in range(groups):
        taken = jnp.take_along_axis(
            cell_table[8 * at : 8 * at + 8, :], low_part, axis=1, mode="promise_in_bounds"
        )
        sent = jnp.where(high_part == at, taken, sent)
    for side in range(4):
        for h in range(2):
            cell_out[side, h : h + 1, :] = sent[4 * h + side : 4 * h + side + 1, :]
    cell_refs = (lambda side: cell_out.at[side], lambda side: cell_in.at[side])
    start(cell_slot, *cell_refs)

    for part, (low, size) in enumerate(CHUNKS):
        for b in range(blocks):
            first_ext[part][b] = guess[part][b].astype(jnp.bfloat16)

    def residual(extended, low, size, b, one, two):
        pair = jnp.concatenate([extended[one], extended[two]], axis=1)
        weight = jnp.concatenate([couple[b, 0], couple[b, 1]], axis=1)
        coupled = nt_dot(pair, weight)
        return (rhs[b, low : low + size, :] - coupled).astype(jnp.bfloat16)

    def smooth(extended, low, size, b):
        return nt_dot(residual(extended, low, size, b, links[0, b], links[1, b]), inverse[b])

    load_links.wait()
    load_couple.wait()
    load_rhs.wait()
    load_inverse.wait()

    spots = [(side, h) for side in range(4) for h in range(halo)]
    spot_blocks = []
    for side, h in spots:
        b = sends[h, side]
        spot_blocks.append((b, links[0, b], links[1, b]))

    def listed(extended, low, size, out):
        resids = [residual(extended, low, size, *at) for at in spot_blocks]
        for (side, h), resid, at in zip(spots, resids, spot_blocks):
            out(side, h, nt_dot(resid, inverse[at[0]]))

    for part, (low, size) in enumerate(CHUNKS):

        def keep(side, h, new):
            second_out[part][side * halo + h] = new.astype(jnp.bfloat16)

        wait_arrived(part, *block_refs(first_out[part], first_ext[part]))
        listed(first_ext[part], low, size, keep)
        start(count + part, *block_refs(second_out[part], second_ext[part]))
    for part, (low, size) in enumerate(CHUNKS):
        for b in range(blocks):
            second_ext[part][b] = smooth(first_ext[part], low, size, b).astype(jnp.bfloat16)

    load_near.wait()
    load_flags.wait()
    wait_arrived(cell_slot, *cell_refs)
    for face in range(6):
        at = slice(face * groups, (face + 1) * groups)
        index = near[at, :]
        own = mode[0] - mode[face // 2 + 1] if face % 2 == 0 else mode[0] + mode[face // 2 + 1]
        rows = [tables[face, g : g + 1, :] for g in range(groups)]
        if face < 4:
            rows = rows + [cell_in[face, h : h + 1, :] for h in range(2)]
            index = jnp.where(index < groups * LANES, index, index - face * 2 * LANES)
        across = pick_lanes(index, rows)
        upwind[at, :] = jnp.where(flags[at, :] == 1, own, across)

    def keep_row(side, h, new):
        face_out[side, h : h + 1, :] = new[0:1, :].astype(jnp.bfloat16).astype(jnp.float32)

    face_refs = (lambda side: face_out.at[side], lambda side: face_in.at[side])
    for part, (low, size) in enumerate(CHUNKS):
        wait_arrived(count + part, *block_refs(second_out[part], second_ext[part]))
        if part == 0:
            listed(second_ext[part], low, size, keep_row)
            start(face_slot, *face_refs)
        for b in range(blocks):
            new = smooth(second_ext[part], low, size, b)
            traces[b, low : low + size, :] = new
            if part == 0:
                face_own[b] = new[0:1, :].astype(jnp.bfloat16).astype(jnp.float32)

    for copy in load_cells:
        copy.wait()
    partial[...] = pick_lanes(faces[...], [face_own[b] for b in range(blocks)])
    wait_arrived(face_slot, *face_refs)
    for side in range(4):
        for h in range(halo):
            face_rows[side * halo + h : side * halo + h + 1, :] = face_in[side, h : h + 1, :]

    for part in range(count):
        wait_sent(part, *block_refs(first_out[part], first_ext[part]))
        wait_sent(count + part, *block_refs(second_out[part], second_ext[part]))
    wait_sent(cell_slot, *cell_refs)
    wait_sent(face_slot, *face_refs)


def section(
    blocks,
    traces,
    partial,
    face_rows,
    upwind,
    faces,
    coeff,
    source,
    modes,
    ratio,
    traces_out,
    modes_out,
    modes_next,
    sem,
):
    write_traces = pltpu.make_async_copy(traces, traces_out, sem.at[0])
    write_traces.start()
    rows = [face_rows[h : h + 1, :] for h in range(face_rows.shape[0])]
    face_trace = pick_lanes(faces[...], rows, blocks, partial[...])
    groups = source.shape[0]
    mode = [modes[pl.ds(m, groups, stride=4), :] for m in range(4)]
    weights = [coeff[f * groups : (f + 1) * groups, :] for f in range(6)]
    values = [face_trace[f * groups : (f + 1) * groups, :] for f in range(6)]
    total = sum(weights[1:], weights[0])
    weighted = [w * v for w, v in zip(weights, values)]
    pressure = (source[...] + sum(weighted[1:], weighted[0])) / total
    flux = [w * (pressure - v) for w, v in zip(weights, values)]
    flow = [flux[f] * upwind[f * groups : (f + 1) * groups, :] for f in range(6)]
    step = ratio[...]
    modes_next[pl.ds(0, groups, stride=4), :] = mode[0] - step * sum(flow[1:], flow[0])
    for m in range(1, 4):
        lo, hi = 2 * m - 2, 2 * m - 1
        volume = 0.5 * (flux[hi] - flux[lo]) * mode[0]
        modes_next[pl.ds(m, groups, stride=4), :] = mode[m] + 3.0 * step * (
            volume - (flow[hi] - flow[lo])
        )
    write_modes = pltpu.make_async_copy(modes_next, modes_out, sem.at[1])
    write_modes.start()
    write_traces.wait()
    write_modes.wait()


def per_device(
    n_wide,
    n_narrow,
    trace_guess,
    trace_rhs,
    block_inverse,
    coupling,
    block_neighbours,
    block_send,
    cell_faces,
    face_coeff,
    cell_source,
    cell_neighbours,
    upwind_flags,
    cell_send,
    saturation,
    step_ratio,
):
    blocks, rows, width = trace_guess.shape[2:]
    halo = block_send.shape[3]
    cells = saturation.shape[3]
    groups = cells // LANES
    side_groups = cell_send.shape[3] // LANES

    def by_tile(x):
        modes, length = x.shape[2:]
        return x.reshape(modes, length // LANES, LANES).transpose(1, 0, 2).reshape(-1, LANES)

    operands = (
        block_neighbours[0, 0].T,
        block_send[0, 0].T,
        trace_guess[0, 0],
        trace_rhs[0, 0],
        block_inverse[0, 0],
        coupling[0, 0],
        cell_faces.reshape(-1, LANES),
        face_coeff.reshape(-1, LANES),
        cell_source.reshape(-1, LANES),
        cell_neighbours.reshape(-1, LANES),
        upwind_flags.reshape(-1, LANES),
        by_tile(cell_send),
        by_tile(saturation),
        step_ratio.reshape(-1, LANES),
    )
    f32, bf16 = jnp.float32, jnp.bfloat16
    extended = blocks + 4 * halo
    slots = 2 * len(CHUNKS) + 2
    scratch = [pltpu.SMEM(x.shape, x.dtype) for x in operands[:2]]
    scratch += [pltpu.VMEM(operands[at].shape, operands[at].dtype) for at in (3, 4, 5, 9, 10, 11)]
    scratch += [
        pltpu.VMEM((6, groups, LANES), f32),
        pltpu.VMEM((8 * groups, LANES), f32),
        pltpu.VMEM((4, side_groups, LANES), f32),
        pltpu.VMEM((4, side_groups, LANES), f32),
        pltpu.VMEM((blocks, 1, width), f32),
        pltpu.VMEM((4, halo, width), f32),
        pltpu.VMEM((4, halo, width), f32),
    ]
    scratch += [pltpu.VMEM((blocks, size, width), f32) for _, size in CHUNKS]
    for leading in (extended, extended, 4 * halo, 4 * halo):
        scratch += [pltpu.VMEM((leading, size, width), bf16) for _, size in CHUNKS]
    scratch += [
        pltpu.SemaphoreType.DMA((13 + len(CHUNKS),)),
        pltpu.SemaphoreType.DMA((slots, 4)),
        pltpu.SemaphoreType.DMA((slots, 4)),
    ]
    cells_shape = (6 * groups, LANES)
    shapes = [(blocks, rows, width), cells_shape, (4 * halo, width), cells_shape]
    kept = [(shape, f32) for shape in shapes]
    kept += [(operands[at].shape, operands[at].dtype) for at in (6, 7, 8, 12, 13)]
    results = pl.pallas_call(
        functools.partial(smooth_kernel, n_wide, n_narrow),
        out_shape=tuple(pltpu.VMEM(*x) for x in kept),
        in_specs=[pl.BlockSpec(memory_space=pltpu.HBM)] * len(operands),
        out_specs=(pl.BlockSpec(memory_space=pltpu.VMEM),) * len(kept),
        scratch_shapes=scratch,
        compiler_params=pltpu.CompilerParams(
            collective_id=0, has_side_effects=True, vmem_limit_bytes=VMEM_LIMIT
        ),
        name="smooth",
    )(*(pltpu.with_memory_space_constraint(x, pltpu.HBM) for x in operands))
    traces, modes = pl.pallas_call(
        functools.partial(section, blocks),
        out_shape=(
            jax.ShapeDtypeStruct(shapes[0], f32),
            jax.ShapeDtypeStruct((4 * groups, LANES), f32),
        ),
        in_specs=[pl.BlockSpec(memory_space=pltpu.VMEM)] * len(kept),
        out_specs=(pl.BlockSpec(memory_space=pl.ANY),) * 2,
        scratch_shapes=[pltpu.VMEM((4 * groups, LANES), f32), pltpu.SemaphoreType.DMA((2,))],
        name="section",
    )(*(pltpu.with_memory_space_constraint(x, pltpu.VMEM) for x in results))
    modes = modes.reshape(groups, 4, LANES).transpose(1, 0, 2).reshape(1, 1, 4, cells)
    return traces[None, None], modes


def solution(mesh):
    def placed(rank):
        return P("wide", "narrow", *([None] * (rank - 2)))

    ranks = (5, 5, 5, 6, 4, 4, 4, 4, 3, 4, 4, 4, 4, 3)
    return jax.shard_map(
        functools.partial(per_device, mesh.shape["wide"], mesh.shape["narrow"]),
        mesh=mesh,
        in_specs=tuple(placed(rank) for rank in ranks),
        out_specs=(placed(5), placed(4)),
        check_vma=False,
    )
```

```python
import functools

import jax
import jax.numpy as jnp
from jax import lax
from jax.experimental import pallas as pl
from jax.experimental.pallas import tpu as pltpu
from jax.sharding import PartitionSpec as P

MESH = pl.DeviceIdType.MESH
LANES = 128
VMEM_LIMIT = 48 * 1024 * 1024
TOP = 8

OPPOSITE = (1, 0, 3, 2)


def nt_dot(a, b):
    return lax.dot_general(a, b, (((1,), (1,)), ((), ())), preferred_element_type=jnp.float32)


def pick_lanes(index, rows, first=0, result=None):
    low = index % LANES
    group = index // LANES
    if result is None:
        result = jnp.zeros(index.shape, jnp.float32)
    for at, row in enumerate(rows, first):
        spread = jnp.broadcast_to(row, index.shape)
        taken = jnp.take_along_axis(spread, low, axis=1, mode="promise_in_bounds")
        result = jnp.where(group == at, taken, result)
    return result


def smooth_kernel(
    n_wide,
    n_narrow,
    links_hbm,
    sends_hbm,
    guess_hbm,
    rhs_hbm,
    inverse_hbm,
    couple_hbm,
    faces_hbm,
    coeff_hbm,
    source_hbm,
    near_hbm,
    flags_hbm,
    outbound_hbm,
    modes_hbm,
    ratio_hbm,
    traces,
    partial,
    face_rows,
    upwind,
    faces,
    coeff,
    source,
    modes,
    ratio,
    links,
    sends,
    rhs,
    inverse,
    couple,
    near,
    flags,
    outbound,
    tables,
    cell_table,
    cell_out,
    cell_in,
    face_own,
    face_out,
    face_in,
    *rest,
):
    top_guess, top_first, top_second, top_first_out, top_second_out, rest = *rest[:5], rest[5:]
    guess, first_ext, second_ext, first_out, second_out, rest = *rest[:5], rest[5:]
    load_sem, send_sem, recv_sem = rest
    blocks = rhs.shape[0]
    halo = sends.shape[0]

    i = lax.axis_index("wide")
    j = lax.axis_index("narrow")
    there = (i > 0, i < n_wide - 1, j > 0, j < n_narrow - 1)
    device = ((i - 1, j), (i + 1, j), (i, j - 1), (i, j + 1))

    def load(at, src, dst):
        copy = pltpu.make_async_copy(src, dst, load_sem.at[at])
        copy.start()
        return copy

    load_sends = load(0, sends_hbm, sends)
    load_top = load(1, guess_hbm.at[:, pl.ds(0, TOP)], top_guess)
    load_guess = load(2, guess_hbm, guess)

    barrier = pltpu.get_barrier_semaphore()
    for side in range(4):

        @pl.when(there[side])
        def _():
            pl.semaphore_signal(barrier, inc=1, device_id=device[side], device_id_type=MESH)

    def remote(src, dst, slot, side):
        return pltpu.make_async_remote_copy(
            src_ref=src,
            dst_ref=dst,
            send_sem=send_sem.at[slot, side],
            recv_sem=recv_sem.at[slot, side],
            device_id=device[side],
            device_id_type=MESH,
        )

    def start(slot, source_of, target_of):
        for side in range(4):

            @pl.when(there[side])
            def _():
                remote(source_of(side), target_of(OPPOSITE[side]), slot, side).start()

    def wait_sent(slot, source_of, target_of):
        for side in range(4):

            @pl.when(there[side])
            def _():
                remote(source_of(side), target_of(OPPOSITE[side]), slot, side).wait_send()

    def wait_arrived(slot, source_of, target_of):
        for side in range(4):

            @pl.when(there[side])
            def _():
                remote(source_of(side), target_of(side), slot, OPPOSITE[side]).wait_recv()

    def block_refs(outgoing, extended):
        return (
            lambda side: outgoing.at[pl.ds(side * halo, halo)],
            lambda side: extended.at[pl.ds(blocks + side * halo, halo)],
        )

    for side in range(4):

        @pl.when(jnp.logical_not(there[side]))
        def _():
            at = pl.ds(blocks + side * halo, halo)
            for extended in (top_first, top_second, first_ext, second_ext):
                extended[at] = jnp.zeros((halo,) + extended.shape[1:], extended.dtype)
            cell_in[side] = jnp.zeros(cell_in.shape[1:], jnp.float32)
            face_in[side] = jnp.zeros(face_in.shape[1:], jnp.float32)

    def rounded(row):
        return row.astype(jnp.bfloat16).astype(jnp.float32)

    top_first_refs = block_refs(top_first_out, top_first)
    top_second_refs = block_refs(top_second_out, top_second)
    first_refs = block_refs(first_out, first_ext)
    second_refs = block_refs(second_out, second_ext)
    spots = [(side, h) for side in range(4) for h in range(halo)]

    load_sends.wait()
    load_top.wait()
    for side, h in spots:
        top_first_out[side * halo + h] = rounded(top_guess[sends[h, side], 0:1, :])
    pl.semaphore_wait(barrier, sum(x.astype(jnp.int32) for x in there))
    start(0, *top_first_refs)
    load_links = load(3, links_hbm, links)
    loads = [
        load(4 + at, src, dst)
        for at, (src, dst) in enumerate(
            (
                (couple_hbm, couple),
                (inverse_hbm, inverse),
                (rhs_hbm, rhs),
                (modes_hbm, modes),
                (outbound_hbm, outbound),
                (near_hbm, near),
                (flags_hbm, flags),
                (faces_hbm, faces),
                (coeff_hbm, coeff),
                (source_hbm, source),
                (ratio_hbm, ratio),
            )
        )
    ]
    load_couple, load_inverse, load_rhs, load_modes, load_outbound, load_near, load_flags = loads[:7]
    load_cells = loads[7:]
    load_guess.wait()
    for side, h in spots:
        first_out[side * halo + h] = guess[sends[h, side]].astype(jnp.bfloat16)
    start(1, *first_refs)

    cell_slot, face_slot = 4, 5
    load_modes.wait()
    load_outbound.wait()
    groups = modes.shape[0] // 4
    mode = [modes[pl.ds(m, groups, stride=4), :] for m in range(4)]
    for face in range(6):
        slope = mode[face // 2 + 1]
        table = mode[0] + slope if face % 2 == 0 else mode[0] - slope
        tables[face] = table
        if face < 4:
            cell_table[pl.ds(OPPOSITE[face], groups, stride=8), :] = table
            cell_table[pl.ds(OPPOSITE[face] + 4, groups, stride=8), :] = table
    index = outbound[...]
    low_part, high_part = index % LANES, index // LANES
    sent = jnp.zeros(index.shape, jnp.float32)
    for at in range(groups):
        taken = jnp.take_along_axis(
            cell_table[8 * at : 8 * at + 8, :], low_part, axis=1, mode="promise_in_bounds"
        )
        sent = jnp.where(high_part == at, taken, sent)
    for side in range(4):
        for h in range(2):
            cell_out[side, h : h + 1, :] = sent[4 * h + side : 4 * h + side + 1, :]
    cell_refs = (lambda side: cell_out.at[side], lambda side: cell_in.at[side])
    start(cell_slot, *cell_refs)

    for b in range(blocks):
        top_first[b] = rounded(top_guess[b, 0:1, :])
        first_ext[b] = guess[b].astype(jnp.bfloat16)

    load_links.wait()
    load_couple.wait()
    load_rhs.wait()
    load_inverse.wait()
    spot_blocks = []
    for side, h in spots:
        b = sends[h, side]
        spot_blocks.append((b, links[0, b], links[1, b]))

    def residual(extended, b, one, two):
        pair = jnp.concatenate([extended[one], extended[two]], axis=1).astype(jnp.bfloat16)
        weight = jnp.concatenate([couple[b, 0], couple[b, 1]], axis=1)
        return (rhs[b, 0 : pair.shape[0], :] - nt_dot(pair, weight)).astype(jnp.bfloat16)

    def listed(extended):
        resids = [residual(extended, *at) for at in spot_blocks]
        return [nt_dot(resid, inverse[at[0]]) for resid, at in zip(resids, spot_blocks)]

    def smooth(extended, b):
        return nt_dot(residual(extended, b, links[0, b], links[1, b]), inverse[b])

    wait_arrived(0, *top_first_refs)
    for (side, h), new in zip(spots, listed(top_first)):
        top_second_out[side * halo + h] = rounded(new)
    start(2, *top_second_refs)
    wait_arrived(1, *first_refs)
    for (side, h), new in zip(spots, listed(first_ext)):
        second_out[side * halo + h] = new.astype(jnp.bfloat16)
    start(3, *second_refs)
    for b in range(blocks):
        new = smooth(first_ext, b)
        top_second[b] = rounded(new[0:1, :])
        second_ext[b] = new.astype(jnp.bfloat16)

    face_refs = (lambda side: face_out.at[side], lambda side: face_in.at[side])
    wait_arrived(2, *top_second_refs)
    for (side, h), new in zip(spots, listed(top_second)):
        face_out[side, h : h + 1, :] = rounded(new)
    start(face_slot, *face_refs)

    load_near.wait()
    load_flags.wait()
    wait_arrived(cell_slot, *cell_refs)
    for face in range(6):
        at = slice(face * groups, (face + 1) * groups)
        index = near[at, :]
        own = mode[0] - mode[face // 2 + 1] if face % 2 == 0 else mode[0] + mode[face // 2 + 1]
        rows = [tables[face, g : g + 1, :] for g in range(groups)]
        if face < 4:
            rows = rows + [cell_in[face, h : h + 1, :] for h in range(2)]
            index = jnp.where(index < groups * LANES, index, index - face * 2 * LANES)
        across = pick_lanes(index, rows)
        upwind[at, :] = jnp.where(flags[at, :] == 1, own, across)

    wait_arrived(3, *second_refs)
    for b in range(blocks):
        new = smooth(second_ext, b)
        traces[b] = new
        face_own[b] = rounded(new[0:1, :])

    for copy in load_cells:
        copy.wait()
    partial[...] = pick_lanes(faces[...], [face_own[b] for b in range(blocks)])
    wait_arrived(face_slot, *face_refs)
    for side in range(4):
        for h in range(halo):
            face_rows[side * halo + h : side * halo + h + 1, :] = face_in[side, h : h + 1, :]

    for slot, refs in enumerate((top_first_refs, first_refs, top_second_refs, second_refs)):
        wait_sent(slot, *refs)
    wait_sent(cell_slot, *cell_refs)
    wait_sent(face_slot, *face_refs)


def section(
    blocks,
    traces,
    partial,
    face_rows,
    upwind,
    faces,
    coeff,
    source,
    modes,
    ratio,
    traces_out,
    modes_out,
    modes_next,
    sem,
):
    write_traces = pltpu.make_async_copy(traces, traces_out, sem.at[0])
    write_traces.start()
    rows = [face_rows[h : h + 1, :] for h in range(face_rows.shape[0])]
    face_trace = pick_lanes(faces[...], rows, blocks, partial[...])
    groups = source.shape[0]
    mode = [modes[pl.ds(m, groups, stride=4), :] for m in range(4)]
    weights = [coeff[f * groups : (f + 1) * groups, :] for f in range(6)]
    values = [face_trace[f * groups : (f + 1) * groups, :] for f in range(6)]
    total = sum(weights[1:], weights[0])
    weighted = [w * v for w, v in zip(weights, values)]
    pressure = (source[...] + sum(weighted[1:], weighted[0])) / total
    flux = [w * (pressure - v) for w, v in zip(weights, values)]
    flow = [flux[f] * upwind[f * groups : (f + 1) * groups, :] for f in range(6)]
    step = ratio[...]
    modes_next[pl.ds(0, groups, stride=4), :] = mode[0] - step * sum(flow[1:], flow[0])
    for m in range(1, 4):
        lo, hi = 2 * m - 2, 2 * m - 1
        volume = 0.5 * (flux[hi] - flux[lo]) * mode[0]
        modes_next[pl.ds(m, groups, stride=4), :] = mode[m] + 3.0 * step * (
            volume - (flow[hi] - flow[lo])
        )
    write_modes = pltpu.make_async_copy(modes_next, modes_out, sem.at[1])
    write_modes.start()
    write_traces.wait()
    write_modes.wait()


def per_device(
    n_wide,
    n_narrow,
    trace_guess,
    trace_rhs,
    block_inverse,
    coupling,
    block_neighbours,
    block_send,
    cell_faces,
    face_coeff,
    cell_source,
    cell_neighbours,
    upwind_flags,
    cell_send,
    saturation,
    step_ratio,
):
    blocks, rows, width = trace_guess.shape[2:]
    halo = block_send.shape[3]
    cells = saturation.shape[3]
    groups = cells // LANES
    side_groups = cell_send.shape[3] // LANES

    def by_tile(x):
        modes, length = x.shape[2:]
        return x.reshape(modes, length // LANES, LANES).transpose(1, 0, 2).reshape(-1, LANES)

    operands = (
        block_neighbours[0, 0].T,
        block_send[0, 0].T,
        trace_guess[0, 0],
        trace_rhs[0, 0],
        block_inverse[0, 0],
        coupling[0, 0],
        cell_faces.reshape(-1, LANES),
        face_coeff.reshape(-1, LANES),
        cell_source.reshape(-1, LANES),
        cell_neighbours.reshape(-1, LANES),
        upwind_flags.reshape(-1, LANES),
        by_tile(cell_send),
        by_tile(saturation),
        step_ratio.reshape(-1, LANES),
    )
    f32, bf16 = jnp.float32, jnp.bfloat16
    extended = blocks + 4 * halo
    scratch = [pltpu.SMEM(x.shape, x.dtype) for x in operands[:2]]
    scratch += [pltpu.VMEM(operands[at].shape, operands[at].dtype) for at in (3, 4, 5, 9, 10, 11)]
    scratch += [
        pltpu.VMEM((6, groups, LANES), f32),
        pltpu.VMEM((8 * groups, LANES), f32),
        pltpu.VMEM((4, side_groups, LANES), f32),
        pltpu.VMEM((4, side_groups, LANES), f32),
        pltpu.VMEM((blocks, 1, width), f32),
        pltpu.VMEM((4, halo, width), f32),
        pltpu.VMEM((4, halo, width), f32),
    ]
    scratch += [pltpu.VMEM((blocks, TOP, width), f32)]
    leadings = (extended, extended, 4 * halo, 4 * halo)
    scratch += [pltpu.VMEM((leading, 1, width), f32) for leading in leadings]
    scratch += [pltpu.VMEM((blocks, rows, width), f32)]
    scratch += [pltpu.VMEM((leading, rows, width), bf16) for leading in leadings]
    scratch += [
        pltpu.SemaphoreType.DMA((15,)),
        pltpu.SemaphoreType.DMA((6, 4)),
        pltpu.SemaphoreType.DMA((6, 4)),
    ]
    cells_shape = (6 * groups, LANES)
    shapes = [(blocks, rows, width), cells_shape, (4 * halo, width), cells_shape]
    kept = [(shape, f32) for shape in shapes]
    kept += [(operands[at].shape, operands[at].dtype) for at in (6, 7, 8, 12, 13)]
    results = pl.pallas_call(
        functools.partial(smooth_kernel, n_wide, n_narrow),
        out_shape=tuple(pltpu.VMEM(*x) for x in kept),
        in_specs=[pl.BlockSpec(memory_space=pltpu.HBM)] * len(operands),
        out_specs=(pl.BlockSpec(memory_space=pltpu.VMEM),) * len(kept),
        scratch_shapes=scratch,
        compiler_params=pltpu.CompilerParams(
            collective_id=0, has_side_effects=True, vmem_limit_bytes=VMEM_LIMIT
        ),
        name="smooth",
    )(*(pltpu.with_memory_space_constraint(x, pltpu.HBM) for x in operands))
    traces, modes = pl.pallas_call(
        functools.partial(section, blocks),
        out_shape=(
            jax.ShapeDtypeStruct(shapes[0], f32),
            jax.ShapeDtypeStruct((4 * groups, LANES), f32),
        ),
        in_specs=[pl.BlockSpec(memory_space=pltpu.VMEM)] * len(kept),
        out_specs=(pl.BlockSpec(memory_space=pl.ANY),) * 2,
        scratch_shapes=[pltpu.VMEM((4 * groups, LANES), f32), pltpu.SemaphoreType.DMA((2,))],
        name="section",
    )(*(pltpu.with_memory_space_constraint(x, pltpu.VMEM) for x in results))
    modes = modes.reshape(groups, 4, LANES).transpose(1, 0, 2).reshape(1, 1, 4, cells)
    return traces[None, None], modes


def solution(mesh):
    def placed(rank):
        return P("wide", "narrow", *([None] * (rank - 2)))

    ranks = (5, 5, 5, 6, 4, 4, 4, 4, 3, 4, 4, 4, 4, 3)
    return jax.shard_map(
        functools.partial(per_device, mesh.shape["wide"], mesh.shape["narrow"]),
        mesh=mesh,
        in_specs=tuple(placed(rank) for rank in ranks),
        out_specs=(placed(5), placed(4)),
        check_vma=False,
    )
```

```python
import functools

import jax
import jax.numpy as jnp
from jax import lax
from jax.experimental import pallas as pl
from jax.experimental.pallas import tpu as pltpu
from jax.sharding import PartitionSpec as P

MESH = pl.DeviceIdType.MESH
LANES = 128
VMEM_LIMIT = 48 * 1024 * 1024
TOP = 8

OPPOSITE = (1, 0, 3, 2)


def nt_dot(a, b):
    return lax.dot_general(a, b, (((1,), (1,)), ((), ())), preferred_element_type=jnp.float32)


def pick_lanes(index, rows, first=0, result=None):
    low = index % LANES
    group = index // LANES
    if result is None:
        result = jnp.zeros(index.shape, jnp.float32)
    for at, row in enumerate(rows, first):
        spread = jnp.broadcast_to(row, index.shape)
        taken = jnp.take_along_axis(spread, low, axis=1, mode="promise_in_bounds")
        result = jnp.where(group == at, taken, result)
    return result


def smooth_kernel(
    n_wide,
    n_narrow,
    links_hbm,
    sends_hbm,
    guess_hbm,
    rhs_hbm,
    inverse_hbm,
    couple_hbm,
    faces_hbm,
    coeff_hbm,
    source_hbm,
    near_hbm,
    flags_hbm,
    outbound_hbm,
    modes_hbm,
    ratio_hbm,
    traces,
    partial,
    face_rows,
    upwind,
    faces,
    coeff,
    source,
    modes,
    ratio,
    links,
    sends,
    rhs,
    inverse,
    couple,
    near,
    flags,
    outbound,
    tables,
    cell_table,
    cell_out,
    cell_in,
    face_own,
    face_out,
    face_in,
    *rest,
):
    top_guess, top_first, top_second, top_first_out, top_second_out, rest = *rest[:5], rest[5:]
    guess, first_ext, second_ext, first_out, second_out, rest = *rest[:5], rest[5:]
    load_sem, send_sem, recv_sem = rest
    blocks = rhs.shape[0]
    halo = sends.shape[0]

    i = lax.axis_index("wide")
    j = lax.axis_index("narrow")
    there = (i > 0, i < n_wide - 1, j > 0, j < n_narrow - 1)
    device = ((i - 1, j), (i + 1, j), (i, j - 1), (i, j + 1))

    def load(at, src, dst):
        copy = pltpu.make_async_copy(src, dst, load_sem.at[at])
        copy.start()
        return copy

    load_sends = load(0, sends_hbm, sends)
    load_top = load(1, guess_hbm.at[:, pl.ds(0, TOP)], top_guess)
    load_guess = load(2, guess_hbm, guess)

    barrier = pltpu.get_barrier_semaphore()
    for side in range(4):

        @pl.when(there[side])
        def _():
            pl.semaphore_signal(barrier, inc=1, device_id=device[side], device_id_type=MESH)

    def remote(src, dst, slot, side):
        return pltpu.make_async_remote_copy(
            src_ref=src,
            dst_ref=dst,
            send_sem=send_sem.at[slot, side],
            recv_sem=recv_sem.at[slot, side],
            device_id=device[side],
            device_id_type=MESH,
        )

    def start(slot, source_of, target_of):
        for side in range(4):

            @pl.when(there[side])
            def _():
                remote(source_of(side), target_of(OPPOSITE[side]), slot, side).start()

    def wait_sent(slot, source_of, target_of):
        for side in range(4):

            @pl.when(there[side])
            def _():
                remote(source_of(side), target_of(OPPOSITE[side]), slot, side).wait_send()

    def wait_arrived(slot, source_of, target_of):
        for side in range(4):

            @pl.when(there[side])
            def _():
                remote(source_of(side), target_of(side), slot, OPPOSITE[side]).wait_recv()

    def block_refs(outgoing, extended):
        return (
            lambda side: outgoing.at[pl.ds(side * halo, halo)],
            lambda side: extended.at[pl.ds(blocks + side * halo, halo)],
        )

    for side in range(4):

        @pl.when(jnp.logical_not(there[side]))
        def _():
            at = pl.ds(blocks + side * halo, halo)
            for extended in (top_first, top_second, first_ext, second_ext):
                extended[at] = jnp.zeros((halo,) + extended.shape[1:], extended.dtype)
            cell_in[side] = jnp.zeros(cell_in.shape[1:], jnp.float32)
            face_in[side] = jnp.zeros(face_in.shape[1:], jnp.float32)

    def rounded(row):
        return row.astype(jnp.bfloat16).astype(jnp.float32)

    top_first_refs = block_refs(top_first_out, top_first)
    top_second_refs = block_refs(top_second_out, top_second)
    first_refs = block_refs(first_out, first_ext)
    second_refs = block_refs(second_out, second_ext)
    spots = [(side, h) for side in range(4) for h in range(halo)]

    load_sends.wait()
    load_top.wait()
    for side, h in spots:
        top_first_out[side * halo + h] = rounded(top_guess[sends[h, side], 0:1, :])
    pl.semaphore_wait(barrier, sum(x.astype(jnp.int32) for x in there))
    start(0, *top_first_refs)
    load_links = load(3, links_hbm, links)
    loads = [
        load(4 + at, src, dst)
        for at, (src, dst) in enumerate(
            (
                (couple_hbm, couple),
                (inverse_hbm, inverse),
                (rhs_hbm, rhs),
                (modes_hbm, modes),
                (outbound_hbm, outbound),
                (near_hbm, near),
                (flags_hbm, flags),
                (faces_hbm, faces),
                (coeff_hbm, coeff),
                (source_hbm, source),
                (ratio_hbm, ratio),
            )
        )
    ]
    load_couple, load_inverse, load_rhs, load_modes, load_outbound, load_near, load_flags = loads[:7]
    load_cells = loads[7:]
    load_guess.wait()
    for side, h in spots:
        first_out[side * halo + h] = guess[sends[h, side]].astype(jnp.bfloat16)
    start(1, *first_refs)

    cell_slot, face_slot = 4, 5
    load_modes.wait()
    load_outbound.wait()
    groups = modes.shape[0] // 4
    mode = [modes[pl.ds(m, groups, stride=4), :] for m in range(4)]
    for face in range(6):
        slope = mode[face // 2 + 1]
        table = mode[0] + slope if face % 2 == 0 else mode[0] - slope
        tables[face] = table
        if face < 4:
            cell_table[pl.ds(OPPOSITE[face], groups, stride=8), :] = table
            cell_table[pl.ds(OPPOSITE[face] + 4, groups, stride=8), :] = table
    index = outbound[...]
    low_part, high_part = index % LANES, index // LANES
    sent = jnp.zeros(index.shape, jnp.float32)
    for at in range(groups):
        taken = jnp.take_along_axis(
            cell_table[8 * at : 8 * at + 8, :], low_part, axis=1, mode="promise_in_bounds"
        )
        sent = jnp.where(high_part == at, taken, sent)
    for side in range(4):
        for h in range(2):
            cell_out[side, h : h + 1, :] = sent[4 * h + side : 4 * h + side + 1, :]
    cell_refs = (lambda side: cell_out.at[side], lambda side: cell_in.at[side])
    start(cell_slot, *cell_refs)

    for b in range(blocks):
        top_first[b] = rounded(top_guess[b, 0:1, :])
        first_ext[b] = guess[b].astype(jnp.bfloat16)

    load_links.wait()
    load_couple.wait()
    load_rhs.wait()
    load_inverse.wait()
    spot_blocks = []
    for side, h in spots:
        b = sends[h, side]
        spot_blocks.append((b, links[0, b], links[1, b]))

    def residual(extended, b, one, two):
        pair = jnp.concatenate([extended[one], extended[two]], axis=1).astype(jnp.bfloat16)
        weight = jnp.concatenate([couple[b, 0], couple[b, 1]], axis=1)
        return (rhs[b, 0 : pair.shape[0], :] - nt_dot(pair, weight)).astype(jnp.bfloat16)

    def listed(extended):
        resids = [residual(extended, *at) for at in spot_blocks]
        return [nt_dot(resid, inverse[at[0]]) for resid, at in zip(resids, spot_blocks)]

    def smooth(extended, b):
        return nt_dot(residual(extended, b, links[0, b], links[1, b]), inverse[b])

    wait_arrived(0, *top_first_refs)
    for (side, h), new in zip(spots, listed(top_first)):
        top_second_out[side * halo + h] = rounded(new)
    start(2, *top_second_refs)
    wait_arrived(1, *first_refs)
    for (side, h), new in zip(spots, listed(first_ext)):
        second_out[side * halo + h] = new.astype(jnp.bfloat16)
    start(3, *second_refs)
    for b in range(blocks):
        new = smooth(first_ext, b)
        top_second[b] = rounded(new[0:1, :])
        second_ext[b] = new.astype(jnp.bfloat16)

    face_refs = (lambda side: face_out.at[side], lambda side: face_in.at[side])
    wait_arrived(2, *top_second_refs)
    for (side, h), new in zip(spots, listed(top_second)):
        face_out[side, h : h + 1, :] = rounded(new)
    start(face_slot, *face_refs)

    load_near.wait()
    load_flags.wait()
    wait_arrived(cell_slot, *cell_refs)
    for face in range(6):
        at = slice(face * groups, (face + 1) * groups)
        index = near[at, :]
        own = mode[0] - mode[face // 2 + 1] if face % 2 == 0 else mode[0] + mode[face // 2 + 1]
        rows = [tables[face, g : g + 1, :] for g in range(groups)]
        if face < 4:
            rows = rows + [cell_in[face, h : h + 1, :] for h in range(2)]
            index = jnp.where(index < groups * LANES, index, index - face * 2 * LANES)
        across = pick_lanes(index, rows)
        upwind[at, :] = jnp.where(flags[at, :] == 1, own, across)

    for b in range(blocks):
        face_own[b] = rounded(smooth(top_second, b))
    for copy in load_cells:
        copy.wait()
    partial[...] = pick_lanes(faces[...], [face_own[b] for b in range(blocks)])

    wait_arrived(3, *second_refs)
    for b in range(blocks):
        traces[b] = smooth(second_ext, b)
    wait_arrived(face_slot, *face_refs)
    for side in range(4):
        for h in range(halo):
            face_rows[side * halo + h : side * halo + h + 1, :] = face_in[side, h : h + 1, :]

    for slot, refs in enumerate((top_first_refs, first_refs, top_second_refs, second_refs)):
        wait_sent(slot, *refs)
    wait_sent(cell_slot, *cell_refs)
    wait_sent(face_slot, *face_refs)


def section(
    blocks,
    traces,
    partial,
    face_rows,
    upwind,
    faces,
    coeff,
    source,
    modes,
    ratio,
    traces_out,
    modes_out,
    modes_next,
    sem,
):
    write_traces = pltpu.make_async_copy(traces, traces_out, sem.at[0])
    write_traces.start()
    rows = [face_rows[h : h + 1, :] for h in range(face_rows.shape[0])]
    face_trace = pick_lanes(faces[...], rows, blocks, partial[...])
    groups = source.shape[0]
    mode = [modes[pl.ds(m, groups, stride=4), :] for m in range(4)]
    weights = [coeff[f * groups : (f + 1) * groups, :] for f in range(6)]
    values = [face_trace[f * groups : (f + 1) * groups, :] for f in range(6)]
    total = sum(weights[1:], weights[0])
    weighted = [w * v for w, v in zip(weights, values)]
    pressure = (source[...] + sum(weighted[1:], weighted[0])) / total
    flux = [w * (pressure - v) for w, v in zip(weights, values)]
    flow = [flux[f] * upwind[f * groups : (f + 1) * groups, :] for f in range(6)]
    step = ratio[...]
    modes_next[pl.ds(0, groups, stride=4), :] = mode[0] - step * sum(flow[1:], flow[0])
    for m in range(1, 4):
        lo, hi = 2 * m - 2, 2 * m - 1
        volume = 0.5 * (flux[hi] - flux[lo]) * mode[0]
        modes_next[pl.ds(m, groups, stride=4), :] = mode[m] + 3.0 * step * (
            volume - (flow[hi] - flow[lo])
        )
    write_modes = pltpu.make_async_copy(modes_next, modes_out, sem.at[1])
    write_modes.start()
    write_traces.wait()
    write_modes.wait()


def per_device(
    n_wide,
    n_narrow,
    trace_guess,
    trace_rhs,
    block_inverse,
    coupling,
    block_neighbours,
    block_send,
    cell_faces,
    face_coeff,
    cell_source,
    cell_neighbours,
    upwind_flags,
    cell_send,
    saturation,
    step_ratio,
):
    blocks, rows, width = trace_guess.shape[2:]
    halo = block_send.shape[3]
    cells = saturation.shape[3]
    groups = cells // LANES
    side_groups = cell_send.shape[3] // LANES

    def by_tile(x):
        modes, length = x.shape[2:]
        return x.reshape(modes, length // LANES, LANES).transpose(1, 0, 2).reshape(-1, LANES)

    operands = (
        block_neighbours[0, 0].T,
        block_send[0, 0].T,
        trace_guess[0, 0],
        trace_rhs[0, 0],
        block_inverse[0, 0],
        coupling[0, 0],
        cell_faces.reshape(-1, LANES),
        face_coeff.reshape(-1, LANES),
        cell_source.reshape(-1, LANES),
        cell_neighbours.reshape(-1, LANES),
        upwind_flags.reshape(-1, LANES),
        by_tile(cell_send),
        by_tile(saturation),
        step_ratio.reshape(-1, LANES),
    )
    f32, bf16 = jnp.float32, jnp.bfloat16
    extended = blocks + 4 * halo
    scratch = [pltpu.SMEM(x.shape, x.dtype) for x in operands[:2]]
    scratch += [pltpu.VMEM(operands[at].shape, operands[at].dtype) for at in (3, 4, 5, 9, 10, 11)]
    scratch += [
        pltpu.VMEM((6, groups, LANES), f32),
        pltpu.VMEM((8 * groups, LANES), f32),
        pltpu.VMEM((4, side_groups, LANES), f32),
        pltpu.VMEM((4, side_groups, LANES), f32),
        pltpu.VMEM((blocks, 1, width), f32),
        pltpu.VMEM((4, halo, width), f32),
        pltpu.VMEM((4, halo, width), f32),
    ]
    scratch += [pltpu.VMEM((blocks, TOP, width), f32)]
    leadings = (extended, extended, 4 * halo, 4 * halo)
    scratch += [pltpu.VMEM((leading, 1, width), f32) for leading in leadings]
    scratch += [pltpu.VMEM((blocks, rows, width), f32)]
    scratch += [pltpu.VMEM((leading, rows, width), bf16) for leading in leadings]
    scratch += [
        pltpu.SemaphoreType.DMA((15,)),
        pltpu.SemaphoreType.DMA((6, 4)),
        pltpu.SemaphoreType.DMA((6, 4)),
    ]
    cells_shape = (6 * groups, LANES)
    shapes = [(blocks, rows, width), cells_shape, (4 * halo, width), cells_shape]
    kept = [(shape, f32) for shape in shapes]
    kept += [(operands[at].shape, operands[at].dtype) for at in (6, 7, 8, 12, 13)]
    results = pl.pallas_call(
        functools.partial(smooth_kernel, n_wide, n_narrow),
        out_shape=tuple(pltpu.VMEM(*x) for x in kept),
        in_specs=[pl.BlockSpec(memory_space=pltpu.HBM)] * len(operands),
        out_specs=(pl.BlockSpec(memory_space=pltpu.VMEM),) * len(kept),
        scratch_shapes=scratch,
        compiler_params=pltpu.CompilerParams(
            collective_id=0, has_side_effects=True, vmem_limit_bytes=VMEM_LIMIT
        ),
        name="smooth",
    )(*(pltpu.with_memory_space_constraint(x, pltpu.HBM) for x in operands))
    traces, modes = pl.pallas_call(
        functools.partial(section, blocks),
        out_shape=(
            jax.ShapeDtypeStruct(shapes[0], f32),
            jax.ShapeDtypeStruct((4 * groups, LANES), f32),
        ),
        in_specs=[pl.BlockSpec(memory_space=pltpu.VMEM)] * len(kept),
        out_specs=(pl.BlockSpec(memory_space=pl.ANY),) * 2,
        scratch_shapes=[pltpu.VMEM((4 * groups, LANES), f32), pltpu.SemaphoreType.DMA((2,))],
        name="section",
    )(*(pltpu.with_memory_space_constraint(x, pltpu.VMEM) for x in results))
    modes = modes.reshape(groups, 4, LANES).transpose(1, 0, 2).reshape(1, 1, 4, cells)
    return traces[None, None], modes


def solution(mesh):
    def placed(rank):
        return P("wide", "narrow", *([None] * (rank - 2)))

    ranks = (5, 5, 5, 6, 4, 4, 4, 4, 3, 4, 4, 4, 4, 3)
    return jax.shard_map(
        functools.partial(per_device, mesh.shape["wide"], mesh.shape["narrow"]),
        mesh=mesh,
        in_specs=tuple(placed(rank) for rank in ranks),
        out_specs=(placed(5), placed(4)),
        check_vma=False,
    )
```
